256 devices in a mesh: seq: 64 (over y, z, core), ch: 4 (over x).
Axes of the slice: x: 4, y: 4, z: 8, core: 2. Of those that a mesh axis runs over, the one named last changes fastest.
Arguments:
- projected: bfloat16 [16384, 3, 8192], P('seq', None, 'ch'), may hold values from -6 to 6
- short_taps: float32 [3, 7, 8192], P(None, None, 'ch'), may hold values from -2 to 2
- filter_taps: float32 [128, 8192], P('seq', 'ch'), may hold values from -1 to 1
- decay: float32 [8192], P('ch'), may hold values from 0.003 to 0.1
- cotangent: bfloat16 [16384, 8192], P('seq', 'ch'), may hold values from -18 to 18
Outputs:
- gated: bfloat16 [16384, 8192], P('seq', 'ch')
- grad_projected: bfloat16 [16384, 3, 8192], P('seq', None, 'ch')
- grad_short: float32 [3, 7, 8192], P(None, None, 'ch')
- grad_filter: float32 [128, 8192], P('seq', 'ch')
The draws below stay inside these ranges and needn't reach their ends.
All inputs are finite; a program needn't handle non-finite values.
Results may differ from the reference program's by a relative error of at most 0.005.
Values may be sent and summed in bfloat16 or wider, within the bound.
A program may use at most 128 MiB of HBM per device.

```python
import math
import jax
import jax.numpy as jnp
from jax import lax

D = 8192
K = 128
FK = 7
TOKENS = 16384


def draw_projected(key, part):
    first, second = jax.random.split(key, 2)
    base = jnp.clip(jax.random.normal(first, (TOKENS, 3, D), jnp.float32), -4.5, 4.5)
    offset = jnp.clip(0.5 * jax.random.normal(second, (1, 3, D), jnp.float32), -1.5, 1.5)
    return (base + offset).astype(jnp.bfloat16)


def draw_cotangent(key, part):
    first = jax.random.fold_in(key, 0)
    third = jax.random.fold_in(key, 2)
    channel = jnp.arange(D, dtype=jnp.float32) / D
    ramp = jnp.power(3.0, channel)[None, :]
    base = jnp.clip(jax.random.normal(first, (TOKENS, D), jnp.float32), -4.0, 4.0)
    offset = jnp.clip(0.5 * jax.random.normal(third, (1, D), jnp.float32), -1.5, 1.5)
    return ((base + offset) * ramp).astype(jnp.bfloat16)


def levels(rng, dims, shards, least, top_value):
    def one(axis_at, blocks):
        steps = jax.random.uniform(jax.random.fold_in(jax.random.fold_in(rng, 6), axis_at), (blocks,), jnp.float32, least / len(shards), top_value / len(shards))
        return jnp.repeat(jnp.exp(steps), dims[axis_at] // blocks).reshape((-1,) + (1,) * (len(dims) - axis_at - 1))

    factor_of = one(*shards[0])
    for cut in shards[1:]:
        factor_of = factor_of * one(*cut)
    return factor_of


def normal_values(own_key, dims, spread, most, cuts=(), kind=jnp.bfloat16):
    values = spread * jax.random.normal(own_key, dims, jnp.float32)
    if cuts:
        values = values * levels(own_key, dims, cuts, -0.22, 0.18)
    return jnp.clip(values, -most, most).astype(kind)


def setup_inputs(seed: int = 0) -> dict:
    key_list = jax.random.split(jax.random.key(seed), 6)
    projected = draw_projected(jax.random.fold_in(key_list[5], 71), 0)
    short_taps = normal_values(key_list[1], (3, FK, D), FK ** -0.5, 2.0, ((2, 4),), jnp.float32)
    filter_taps = normal_values(key_list[2], (K, D), (K // 3) ** -0.5, 1.0, ((0, 64), (1, 4)), jnp.float32)
    decay = jnp.clip(jnp.exp(math.log(0.1) - 3.506558 * jax.random.uniform(key_list[3], (D,), jnp.float32) ** levels(key_list[3], (D,), ((0, 4),), -0.2, 0.2)), 0.003, 0.1)
    cotangent = draw_cotangent(jax.random.fold_in(key_list[5], 71), 0)
    return dict(projected=projected, short_taps=short_taps, filter_taps=filter_taps, decay=decay, cotangent=cotangent)


def causal_short(proj, short):
    length = proj.shape[0]
    padded = jnp.concatenate([jnp.zeros((FK - 1,) + proj.shape[1:], proj.dtype), proj], axis=0)
    total = jnp.zeros_like(proj)
    for lag in range(FK):
        total = total + short[:, lag, :] * padded[FK - 1 - lag:FK - 1 - lag + length]
    return total

def long_conv(mixed, kernel):
    length = mixed.shape[0]
    extent = 2 * length
    spectrum = jnp.fft.rfft(mixed, n=extent, axis=0) * jnp.fft.rfft(kernel, n=extent, axis=0)
    return jnp.fft.irfft(spectrum, n=extent, axis=0)[:length]

def forward(proj, short, filt, decay):
    feat = causal_short(proj, short)
    lags = jnp.arange(K, dtype=jnp.float32)
    kernel = filt * jnp.exp(-decay[None, :] * lags[:, None])
    mixed = feat[:, 1, :] * feat[:, 2, :]
    return feat[:, 0, :] * long_conv(mixed, kernel)

def one_block(pieces):
    proj, short, filt, decay, cot = pieces

    def partial_forward(proj_in, short_in, filt_in):
        return forward(proj_in, short_in, filt_in, decay)
    output, pullback = jax.vjp(partial_forward, proj.astype(jnp.float32), short, filt)
    grads = pullback(cot.astype(jnp.float32))
    return (output.astype(jnp.bfloat16), grads[0].astype(jnp.bfloat16), grads[1], grads[2])

def reference(projected, short_taps, filter_taps, decay, cotangent):
    width = 512 if D % 512 == 0 else D
    blocks = D // width
    length = projected.shape[0]
    proj_b = jnp.moveaxis(projected.reshape(length, 3, blocks, width), 2, 0)
    short_b = jnp.moveaxis(short_taps.reshape(3, FK, blocks, width), 2, 0)
    filt_b = jnp.moveaxis(filter_taps.reshape(K, blocks, width), 1, 0)
    decay_b = decay.reshape(blocks, width)
    cot_b = jnp.moveaxis(cotangent.reshape(length, blocks, width), 1, 0)
    out_b, gproj_b, gshort_b, gfilt_b = lax.map(one_block, (proj_b, short_b, filt_b, decay_b, cot_b))
    gated = jnp.moveaxis(out_b, 0, 1).reshape(length, D)
    grad_projected = jnp.moveaxis(gproj_b, 0, 2).reshape(length, 3, D)
    short_raw = jnp.moveaxis(gshort_b, 0, 2).reshape(3, FK, D)
    filter_raw = jnp.moveaxis(gfilt_b, 0, 1).reshape(K, D)
    total = jnp.sum(filter_raw * filter_raw) + jnp.sum(short_raw * short_raw)
    limit = math.sqrt(K * D + 3 * FK * D)
    scale = jnp.minimum(1.0, limit / jnp.sqrt(total))
    return (gated, grad_projected, scale * short_raw, scale * filter_raw)
```

```python
import functools
import math

import jax
import jax.numpy as jnp
import ml_dtypes
import numpy as np
from jax import lax
from jax.experimental import pallas as pl
from jax.experimental.pallas import tpu as pltpu
from jax.sharding import PartitionSpec as P

K = 128
FK = 7
HALO = FK - 1
NY = 4
NZ = 8
B = 128
N = 2 * B
W = 256
LANES = 128
SUB = 8
R = B // SUB
F32 = jnp.float32
BF16 = jnp.bfloat16
MESH = pl.DeviceIdType.MESH


def constants(per_device):
    place = np.arange(B)
    time = (place % SUB) * R + place // SUB
    order = np.zeros((B, B))
    order[place, time] = 1.0
    freq = np.concatenate([np.arange(0, B, 2), np.arange(1, B, 2)])
    sign = np.where(freq % 2 == 0, 1.0, -1.0)
    theta = 2.0 * np.pi * (freq + 0.5) / N
    slot = np.arange(K)
    end = slot % per_device
    rest = slot // per_device
    z, y, core = rest % NZ, (rest // NZ) % NY, rest // (NZ * NY)
    tap = ((y * NZ + z) * 2 + core) * per_device + end

    def forward(times):
        angle = theta[:, None] * times[None, :]
        full = np.concatenate([np.cos(angle), -np.sin(angle)], axis=0)
        high = full.astype(ml_dtypes.bfloat16)
        low = (full - high.astype(np.float64)).astype(ml_dtypes.bfloat16)
        return np.concatenate([high, low], axis=1)

    def inverse(times):
        angle = times[:, None] * theta[None, :]
        return np.concatenate([np.cos(angle), -np.sin(angle)], axis=1) * (2.0 / N)

    angle = tap[:, None] * theta[None, :]
    inv_corr = np.concatenate([np.sin(angle) * sign, np.cos(angle) * sign], axis=1) * (2.0 / N)
    as_bf16 = lambda value: np.asarray(value).astype(ml_dtypes.bfloat16)
    return tuple(
        as_bf16(value)
        for value in (
            order,
            order.T,
            forward(time),
            forward(tap),
            inverse(B + time),
            inverse(time),
            inv_corr,
        )
    )


def dot(a, b):
    return jnp.dot(a, b, preferred_element_type=F32)


def twice(value):
    return jnp.concatenate([value, value], axis=0)


def ahead(p, q):
    return [p[0] + q[2], p[1] - q[3], p[2] - q[0], p[3] + q[1]]


class Sems:
    def __init__(self, ref):
        self.ref, self.used = ref, 0

    def take(self, count):
        first, self.used = self.used, self.used + count
        return first


SEM_COUNT = 256


def kernel(
    nseq,
    nch,
    proj,
    cot,
    short_taps,
    taps,
    decay,
    order,
    order_t,
    fwd,
    fwd_taps,
    inv_conv,
    inv_grad,
    inv_corr,
    gated_out,
    gproj_out,
    short_out,
    filter_out,
    xn,
    cn,
    xhalo,
    xp,
    feat,
    cotp,
    mx,
    gf,
    hx,
    hg,
    spec,
    hspec,
    prod,
    prod2,
    khat,
    kbf,
    kmine,
    kgather,
    kflat,
    conv,
    gb,
    gfe,
    ghsend,
    ghrecv,
    og,
    op,
    fr,
    frc,
    fry_f,
    fry,
    fryr,
    frz_f,
    frz,
    frzr,
    frfin,
    sr,
    src_,
    sry,
    sryr,
    srz,
    srzr,
    ag,
    sqx,
    sqz,
    sqy,
    sqc,
    sem_ref,
):
    cols = cot.shape[1]
    nchunk = cols // W
    cbn = cols // LANES
    per_device = taps.shape[0]
    slab = per_device * cbn
    half = NY * NZ
    me = lax.axis_index("seq")
    ch = lax.axis_index("ch")
    core = lax.rem(me, 2)
    z = lax.rem(me // 2, NZ)
    y = me // (2 * NZ)
    other = 1 - core
    seq_at = lambda yy, zz, cc: (yy * NZ + zz) * 2 + cc
    nxt = lax.rem(me + 1, nseq)
    prv = lax.rem(me + nseq - 1, nseq)
    at_z = [lax.rem(z + o, NZ) for o in range(NZ)]
    at_y = [lax.rem(y + o, NY) for o in range(NY)]
    at_x = [lax.rem(ch + o, nch) for o in range(nch)]
    from_z = [lax.rem(z + NZ - o, NZ) for o in range(NZ)]
    from_y = [lax.rem(y + NY - o, NY) for o in range(NY)]
    from_x = [lax.rem(ch + nch - o, nch) for o in range(nch)]
    dev_z = lambda o: (seq_at(y, at_z[o], core), ch)
    dev_y = lambda o: (seq_at(at_y[o], z, core), ch)
    dev_x = lambda o: (me, at_x[o])
    dev_c = (seq_at(y, z, other), ch)
    dev_next, dev_prev = (nxt, ch), (prv, ch)
    sems = Sems(sem_ref)
    sends = []

    def remote(src, dst, send, recv, dev):
        return pltpu.make_async_remote_copy(
            src_ref=src,
            dst_ref=dst,
            send_sem=sem_ref.at[send],
            recv_sem=sem_ref.at[recv],
            device_id=dev,
            device_id_type=MESH,
        )

    def send(src, dst, ss, rs, dev):
        copy = remote(src, dst, ss, rs, dev)
        copy.start()
        sends.append(copy)

    def got(dst, ss, rs):
        remote(dst, dst, ss, rs, dev_next).wait_recv()

    s_in = sems.take(2 * nchunk)

    def load(c):
        at = pl.ds(pl.multiple_of(c * W, W), W)
        return (
            pltpu.make_async_copy(proj.at[:, :, at], xn.at[:, :, at], sem_ref.at[s_in + 2 * c]),
            pltpu.make_async_copy(cot.at[:, at], cn.at[:, at], sem_ref.at[s_in + 2 * c + 1]),
        )

    for c in range(nchunk):
        for copy in load(c):
            copy.start()

    barrier = pltpu.get_barrier_semaphore()
    partners = [dev_next, dev_prev, dev_c]
    partners += [dev_z(o) for o in range(1, NZ)]
    partners += [dev_y(o) for o in range(1, NY)]
    partners += [dev_x(o) for o in range(1, nch)]
    for dev in partners:
        pl.semaphore_signal(barrier, inc=1, device_id=dev, device_id_type=MESH)

    for e in range(per_device):
        lag = (me * per_device + e).astype(F32)
        fall = jnp.exp(-decay[...] * lag)
        for cb in range(cbn):
            row = taps[e : e + 1, cb * LANES : (cb + 1) * LANES]
            kflat[e * cbn + cb : e * cbn + cb + 1, :] = row
        part = pl.ds(e * cbn, cbn)
        kflat[part, :] = kflat[part, :] * fall
    slot = core * half + y * NZ + z
    slot_at = lambda cc, yy, zz: pl.ds(
        pl.multiple_of((cc * half + yy * NZ + zz) * slab, slab), slab
    )
    bundle_at = lambda cc, yy: pl.ds(
        pl.multiple_of((cc * half + yy * NZ) * slab, NZ * slab), NZ * slab
    )
    half_at = lambda cc: pl.ds(pl.multiple_of(cc * half * slab, half * slab), half * slab)
    kmine[...] = kflat[0:slab, :].astype(BF16)
    kgather[slot_at(core, y, z), :] = kmine[...]

    pl.semaphore_wait(barrier, len(partners))

    s_xh = sems.take(2)
    tail = proj.shape[1] - SUB
    send(proj.at[:, pl.ds(tail, SUB), :], xhalo, s_xh, s_xh + 1, dev_next)
    s_kz = sems.take(2 * NZ)
    for o in range(1, NZ):
        send(kmine, kgather.at[slot_at(core, y, z)], s_kz + o, s_kz + NZ + o, dev_z(o))

    first = jnp.where(me > 0, 1.0, 0.0).astype(F32)
    last = jnp.where(me < nseq - 1, 1.0, 0.0).astype(F32)
    row_id = lax.broadcasted_iota(jnp.int32, (HALO, SUB, LANES), 1)
    top, bottom = row_id == 0, row_id == SUB - 1
    rows = [slice(0, B), slice(B, 2 * B)]

    def tap_rows(i, at):
        return [jnp.broadcast_to(short_taps[i, j : j + 1, at], (SUB, LANES)) for j in range(FK)]

    s_hx = sems.take(2 * nchunk)
    s_hg = sems.take(2 * nchunk)

    def halo_x(c):
        at = pl.ds(pl.multiple_of(c * W, W), W)
        return remote(mx.at[pl.ds(B, B), at], hx.at[:, at], s_hx + c, s_hx + nchunk + c, dev_next)

    def halo_g(c):
        at = pl.ds(pl.multiple_of(c * W, W), W)
        return remote(gf.at[pl.ds(0, B), at], hg.at[:, at], s_hg + c, s_hg + nchunk + c, dev_prev)

    got(xhalo, s_xh, s_xh + 1)

    def features(c, carry):
        for copy in load(c):
            copy.wait()
        at = pl.ds(pl.multiple_of(c * W, W), W)
        for b in range(2):
            for i in range(3):
                xp[i, b, HALO:, :, at] = dot(order[...], xn[i, rows[b], at]).reshape(R, SUB, W)
            cotp[b, :, :, at] = dot(order[...], cn[rows[b], at]).reshape(R, SUB, W)
        for sub in range(W // LANES):
            ls = pl.ds(pl.multiple_of(c * W + sub * LANES, LANES), LANES)
            for i in range(3):
                weights = tap_rows(i, ls)
                head = xhalo[i, :, ls].astype(F32) * first
                before = jnp.concatenate(
                    [
                        jnp.broadcast_to(head[2 + q : 3 + q, :], (SUB, LANES))[None]
                        for q in range(HALO)
                    ],
                    axis=0,
                )
                for b in range(2):
                    turned = pltpu.roll(xp[i, b, R:, :, ls], 1, axis=1)
                    xp[i, b, :HALO, :, ls] = jnp.where(top, before, turned)
                    before = turned
                    total = weights[0] * xp[i, b, HALO:, :, ls]
                    for j in range(1, FK):
                        total = total + weights[j] * xp[i, b, HALO - j : HALO - j + R, :, ls]
                    feat[i, b, :, :, ls] = total
            for b in range(2):
                mixed = feat[1, b, :, :, ls] * feat[2, b, :, :, ls]
                mx[rows[b], ls] = mixed.reshape(B, LANES).astype(BF16)
                grad = cotp[b, :, :, ls] * feat[0, b, :, :, ls]
                gf[rows[b], ls] = grad.reshape(B, LANES).astype(BF16)
        halo_x(c).start()
        halo_g(c).start()
        for b in range(2):
            spec[b, :, at] = dot(fwd[...], twice(mx[rows[b], at]))
            spec[2 + b, :, at] = dot(fwd[...], twice(gf[rows[b], at]))
        return carry

    lax.fori_loop(0, nchunk, features, 0)

    s_ky = sems.take(2 * NY)
    for o in range(1, NZ):
        got(kgather.at[slot_at(core, y, from_z[o])], s_kz + o, s_kz + NZ + o)
    for o in range(1, NY):
        block = kgather.at[bundle_at(core, y)]
        send(block, block, s_ky + o, s_ky + NY + o, dev_y(o))

    quarter = B // 2

    def quads(ref, rs, ls):
        return [ref[pl.ds(q * quarter + rs, 32), ls] for q in range(4)]

    def correlate(c, carry):
        at = pl.ds(pl.multiple_of(c * W, W), W)
        halo_x(c).wait_recv()
        halo_g(c).wait_recv()
        hspec[0] = dot(fwd[...], twice(hx[:, at]))
        hspec[1] = dot(fwd[...], twice(hg[:, at]))
        for sub in range(W // LANES):
            here = slice(sub * LANES, (sub + 1) * LANES)
            ls = pl.ds(pl.multiple_of(c * W + sub * LANES, LANES), LANES)
            for rs in range(0, quarter, 32):
                hq = [v * first for v in quads(hspec.at[0], rs, here)]
                gq = [v * last for v in quads(hspec.at[1], rs, here)]
                a, b, ga, gbq = [quads(spec.at[q], rs, ls) for q in range(4)]
                x0, x1 = ahead(hq, a), ahead(a, b)
                g0, g1 = ahead(ga, gbq), ahead(gbq, gq)
                for q in range(4):
                    part = pl.ds(q * quarter + rs, 32)
                    spec[0, part, ls] = x0[q]
                    spec[1, part, ls] = x1[q]
                    spec[2, part, ls] = g0[q]
                    spec[3, part, ls] = g1[q]
                for q in range(2):
                    re = ga[q] * x0[q] + ga[q + 2] * x0[q + 2]
                    re = re + (gbq[q] * x1[q] + gbq[q + 2] * x1[q + 2])
                    im = ga[q + 2] * x0[q] - ga[q] * x0[q + 2]
                    im = im + (gbq[q + 2] * x1[q] - gbq[q] * x1[q + 2])
                    prod[0, pl.ds(q * quarter + rs, 32), here] = re.astype(BF16)
                    prod[0, pl.ds((q + 2) * quarter + rs, 32), here] = im.astype(BF16)
        corr = dot(inv_corr[...], prod[0])
        for sub in range(W // LANES):
            cb = c * (W // LANES) + sub
            fr[pl.ds(cb, K, stride=cbn), :] = corr[:, sub * LANES : (sub + 1) * LANES]
        return carry

    lax.fori_loop(0, nchunk, correlate, 0)

    s_fc = sems.take(2)
    send(fr.at[half_at(other)], frc, s_fc, s_fc + 1, dev_c)
    s_kc = sems.take(2)
    for o in range(1, NY):
        got(kgather.at[bundle_at(core, from_y[o])], s_ky + o, s_ky + NY + o)
    block = kgather.at[half_at(core)]
    send(block, block, s_kc, s_kc + 1, dev_c)
    got(kgather.at[half_at(other)], s_kc, s_kc + 1)
    kflat[...] = kgather[...].astype(F32)

    s_og = sems.take(nchunk)

    def store_gated(c):
        at = pl.ds(pl.multiple_of(c * W, W), W)
        return pltpu.make_async_copy(og.at[:, at], gated_out.at[:, at], sem_ref.at[s_og + c])

    def filters(c, carry):
        at = pl.ds(pl.multiple_of(c * W, W), W)
        for sub in range(W // LANES):
            cb = c * (W // LANES) + sub
            here = slice(sub * LANES, (sub + 1) * LANES)
            kbf[:, here] = kflat[pl.ds(cb, K, stride=cbn), :].astype(BF16)
        khat[...] = dot(fwd_taps[...], twice(kbf[...]))
        for sub in range(W // LANES):
            here = slice(sub * LANES, (sub + 1) * LANES)
            ls = pl.ds(pl.multiple_of(c * W + sub * LANES, LANES), LANES)
            for rs in range(0, B, 32):
                re, im = pl.ds(rs, 32), pl.ds(B + rs, 32)
                kr, ki = khat[re, here], khat[im, here]
                for b in range(2):
                    xr, xi = spec[b, re, ls], spec[b, im, ls]
                    prod[b, re, here] = (kr * xr - ki * xi).astype(BF16)
                    prod[b, im, here] = (kr * xi + ki * xr).astype(BF16)
                    xr, xi = spec[2 + b, re, ls], spec[2 + b, im, ls]
                    prod2[b, re, here] = (kr * xr + ki * xi).astype(BF16)
                    prod2[b, im, here] = (kr * xi - ki * xr).astype(BF16)
        for b in range(2):
            conv[0, b] = dot(inv_conv[...], prod[b]).reshape(R, SUB, W)
            conv[1, b] = dot(inv_grad[...], prod2[b]).reshape(R, SUB, W)
        for sub in range(W // LANES):
            here = slice(sub * LANES, (sub + 1) * LANES)
            ls = pl.ds(pl.multiple_of(c * W + sub * LANES, LANES), LANES)
            for b in range(2):
                filtered, mixed_grad = conv[0, b, :, :, here], conv[1, b, :, :, here]
                gate = feat[0, b, :, :, ls] * filtered
                gb[rows[b], here] = gate.reshape(B, LANES).astype(BF16)
                gfe[0, b, :, :, ls] = cotp[b, :, :, ls] * filtered
                gfe[1, b, :, :, ls] = mixed_grad * feat[2, b, :, :, ls]
                gfe[2, b, :, :, ls] = mixed_grad * feat[1, b, :, :, ls]
            zero = jnp.zeros((1, LANES), F32)
            for i in range(3):
                parts = []
                for j in range(FK):
                    both = [
                        jnp.sum(
                            gfe[i, b, :, :, ls] * xp[i, b, HALO - j : HALO - j + R, :, ls], axis=0
                        )
                        for b in range(2)
                    ]
                    parts.append(jnp.sum(both[0] + both[1], axis=0, keepdims=True))
                cb = c * (W // LANES) + sub
                at_slab = pl.ds(pl.multiple_of((i * cbn + cb) * SUB, SUB), SUB)
                sr[at_slab, :] = jnp.concatenate(parts + [zero], axis=0)
                heads = [gfe[i, 0, q, 0:1, ls] for q in range(HALO)]
                ghsend[i, :, ls] = jnp.concatenate(heads + [zero, zero], axis=0).astype(BF16)
        for b in range(2):
            og[rows[b], at] = dot(order_t[...], gb[rows[b], :]).astype(BF16)
        store_gated(c).start()
        return carry

    spare = nseq - 3 * cbn
    if spare > 0:
        sr[pl.ds(3 * cbn * SUB, spare * SUB), :] = jnp.zeros((spare * SUB, LANES), F32)

    cut = nchunk // 2
    lax.fori_loop(0, cut, filters, 0)

    got(frc, s_fc, s_fc + 1)
    fry_f[...] = fr[half_at(core), :] + frc[...]
    fry[...] = fry_f[...].astype(BF16)
    s_fy = sems.take(2 * NY)
    quart = NZ * slab
    quart_at = lambda yy: pl.ds(pl.multiple_of(yy * quart, quart), quart)
    for o in range(1, NY):
        send(fry.at[quart_at(at_y[o])], fryr.at[o - 1], s_fy + o, s_fy + NY + o, dev_y(o))

    lax.fori_loop(cut, nchunk, filters, 0)

    s_gh = sems.take(2)
    send(ghsend, ghrecv, s_gh, s_gh + 1, dev_prev)
    s_sc = sems.take(2)
    shalf = half * SUB
    shalf_at = lambda cc: pl.ds(pl.multiple_of(cc * shalf, shalf), shalf)
    send(sr.at[shalf_at(other)], src_, s_sc, s_sc + 1, dev_c)

    for o in range(1, NY):
        got(fryr.at[o - 1], s_fy + o, s_fy + NY + o)
    total = fry_f[quart_at(y), :]
    for o in range(1, NY):
        total = total + fryr[o - 1].astype(F32)
    frz_f[...] = total
    frz[...] = total.astype(BF16)
    s_fz = sems.take(2 * NZ)
    slab_at = lambda zz: pl.ds(pl.multiple_of(zz * slab, slab), slab)
    for o in range(1, NZ):
        send(frz.at[slab_at(at_z[o])], frzr.at[o - 1], s_fz + o, s_fz + NZ + o, dev_z(o))

    got(src_, s_sc, s_sc + 1)
    sry[...] = sr[shalf_at(core), :] + src_[...]
    s_sy = sems.take(2 * NY)
    sq_rows = NZ * SUB
    sq_at = lambda yy: pl.ds(pl.multiple_of(yy * sq_rows, sq_rows), sq_rows)
    for o in range(1, NY):
        send(sry.at[sq_at(at_y[o])], sryr.at[o - 1], s_sy + o, s_sy + NY + o, dev_y(o))

    got(ghrecv, s_gh, s_gh + 1)
    s_op = sems.take(nchunk)

    def store_gproj(c):
        at = pl.ds(pl.multiple_of(c * W, W), W)
        return pltpu.make_async_copy(op.at[:, :, at], gproj_out.at[:, :, at], sem_ref.at[s_op + c])

    def backward(c, carry):
        at = pl.ds(pl.multiple_of(c * W, W), W)
        for i in range(3):
            for sub in range(W // LANES):
                here = slice(sub * LANES, (sub + 1) * LANES)
                ls = pl.ds(pl.multiple_of(c * W + sub * LANES, LANES), LANES)
                weights = tap_rows(i, ls)
                foot = ghrecv[i, :, ls].astype(F32) * last
                after = jnp.concatenate(
                    [
                        jnp.broadcast_to(foot[q : q + 1, :], (SUB, LANES))[None]
                        for q in range(HALO)
                    ],
                    axis=0,
                )
                for b in (1, 0):
                    turned = pltpu.roll(gfe[i, b, :HALO, :, ls], SUB - 1, axis=1)
                    full = jnp.concatenate(
                        [gfe[i, b, :, :, ls], jnp.where(bottom, after, turned)], axis=0
                    )
                    after = turned
                    total = weights[0] * full[:R]
                    for j in range(1, FK):
                        total = total + weights[j] * full[j : j + R]
                    gb[rows[b], here] = total.reshape(B, LANES).astype(BF16)
            for b in range(2):
                op[i, rows[b], at] = dot(order_t[...], gb[rows[b], :]).astype(BF16)
        store_gproj(c).start()
        return carry

    steps = [nchunk * k // 4 for k in range(5)]
    lax.fori_loop(steps[0], steps[1], backward, 0)

    for o in range(1, NY):
        got(sryr.at[o - 1], s_sy + o, s_sy + NY + o)
    total = sry[sq_at(y), :]
    for o in range(1, NY):
        total = total + sryr[o - 1]
    srz[...] = total
    s_sz = sems.take(2 * NZ)
    one_at = lambda zz: pl.ds(pl.multiple_of(zz * SUB, SUB), SUB)
    for o in range(1, NZ):
        send(srz.at[one_at(at_z[o])], srzr.at[o - 1], s_sz + o, s_sz + NZ + o, dev_z(o))

    lax.fori_loop(steps[1], steps[2], backward, 0)

    for o in range(1, NZ):
        got(frzr.at[o - 1], s_fz + o, s_fz + NZ + o)
    total = frz_f[slab_at(z), :]
    for o in range(1, NZ):
        total = total + frzr[o - 1].astype(F32)
    for e in range(per_device):
        lag = (me * per_device + e).astype(F32)
        part = pl.ds(e * cbn, cbn)
        frfin[part, :] = total[e * cbn : (e + 1) * cbn, :] * jnp.exp(-decay[...] * lag)

    for o in range(1, NZ):
        got(srzr.at[o - 1], s_sz + o, s_sz + NZ + o)
    mine = srz[one_at(z), :]
    for o in range(1, NZ):
        mine = mine + srzr[o - 1]
    s_at = lambda cc, yy, zz: pl.ds(pl.multiple_of((cc * half + yy * NZ + zz) * SUB, SUB), SUB)
    s_bundle = lambda cc, yy: pl.ds(
        pl.multiple_of((cc * half + yy * NZ) * SUB, NZ * SUB), NZ * SUB
    )
    ag[s_at(core, y, z), :] = mine
    square = mine * mine
    whole = frfin[...]
    square = square + jnp.sum((whole * whole).reshape(slab // SUB, SUB, LANES), axis=0)
    s_az = sems.take(2 * NZ)
    for o in range(1, NZ):
        block = ag.at[s_at(core, y, z)]
        send(block, block, s_az + o, s_az + NZ + o, dev_z(o))

    def share(buf, value, index, base, count, to, source):
        buf[index] = value
        for o in range(1, count):
            send(buf.at[index], buf.at[index], base + o, base + count + o, to(o))

    def gathered(buf, base, count, source):
        for o in range(1, count):
            got(buf.at[source[o]], base + o, base + count + o)
        value = buf[0]
        for k in range(1, count):
            value = value + buf[k]
        return value

    s_qx = sems.take(2 * nch)
    share(sqx, square, ch, s_qx, nch, dev_x, from_x)
    lax.fori_loop(steps[2], steps[3], backward, 0)
    square = gathered(sqx, s_qx, nch, from_x)
    s_qz = sems.take(2 * NZ)
    share(sqz, square, z, s_qz, NZ, dev_z, from_z)

    s_ay = sems.take(2 * NY)
    for o in range(1, NZ):
        got(ag.at[s_at(core, y, from_z[o])], s_az + o, s_az + NZ + o)
    for o in range(1, NY):
        block = ag.at[s_bundle(core, y)]
        send(block, block, s_ay + o, s_ay + NY + o, dev_y(o))

    lax.fori_loop(steps[3], steps[4], backward, 0)

    square = gathered(sqz, s_qz, NZ, from_z)
    s_qy = sems.take(2 * NY)
    share(sqy, square, y, s_qy, NY, dev_y, from_y)

    s_ac = sems.take(2)
    for o in range(1, NY):
        got(ag.at[s_bundle(core, from_y[o])], s_ay + o, s_ay + NY + o)
    block = ag.at[shalf_at(core)]
    send(block, block, s_ac, s_ac + 1, dev_c)

    square = gathered(sqy, s_qy, NY, from_y)
    s_qc = sems.take(2)
    sqc[core] = square
    send(sqc.at[core], sqc.at[core], s_qc, s_qc + 1, dev_c)
    got(sqc.at[other], s_qc, s_qc + 1)
    square = sqc[0] + sqc[1]
    sums = jnp.sum(jnp.sum(square, axis=0, keepdims=True), axis=1, keepdims=True)
    channels = cols * nch
    limit = math.sqrt(K * channels + 3 * FK * channels)
    scale = jnp.minimum(1.0, limit / jnp.sqrt(sums))
    for e in range(per_device):
        for cb in range(cbn):
            value = frfin[e * cbn + cb : e * cbn + cb + 1, :] * scale
            filter_out[e : e + 1, cb * LANES : (cb + 1) * LANES] = value
    got(ag.at[shalf_at(other)], s_ac, s_ac + 1)
    for i in range(3):
        for cb in range(cbn):
            first_row = (i * cbn + cb) * SUB
            value = ag[first_row : first_row + FK, :] * scale
            short_out[i, :, cb * LANES : (cb + 1) * LANES] = value

    def finish(c, carry):
        halo_x(c).wait_send()
        halo_g(c).wait_send()
        store_gated(c).wait()
        store_gproj(c).wait()
        return carry

    lax.fori_loop(0, nchunk, finish, 0)
    for copy in sends:
        copy.wait_send()


def shards(nseq, nch, projected, short_taps, filter_taps, decay, cotangent):
    length, cols = cotangent.shape
    per_device = filter_taps.shape[0]
    cbn = cols // LANES
    slab = per_device * cbn
    half = NY * NZ
    nchunk = cols // W
    vmem = pltpu.VMEM
    consts = [jnp.asarray(value) for value in constants(per_device)]
    any_spec = pl.BlockSpec(memory_space=pl.ANY)
    vmem_spec = pl.BlockSpec(memory_space=pltpu.VMEM)
    scratch = [
        vmem((3, length, cols), BF16),
        vmem((length, cols), BF16),
        vmem((3, SUB, cols), BF16),
        vmem((3, 2, R + HALO, SUB, cols), F32),
        vmem((3, 2, R, SUB, cols), F32),
        vmem((2, R, SUB, cols), F32),
        vmem((length, cols), BF16),
        vmem((length, cols), BF16),
        vmem((B, cols), BF16),
        vmem((B, cols), BF16),
        vmem((4, N, cols), F32),
        vmem((2, N, W), F32),
        vmem((2, N, W), BF16),
        vmem((2, N, W), BF16),
        vmem((N, W), F32),
        vmem((K, W), BF16),
        vmem((slab, LANES), BF16),
        vmem((K * cbn, LANES), BF16),
        vmem((K * cbn, LANES), F32),
        vmem((2, 2, R, SUB, W), F32),
        vmem((length, W), BF16),
        vmem((3, 2, R, SUB, cols), F32),
        vmem((3, SUB, cols), BF16),
        vmem((3, SUB, cols), BF16),
        vmem((length, cols), BF16),
        vmem((3, length, cols), BF16),
        vmem((K * cbn, LANES), F32),
        vmem((half * slab, LANES), F32),
        vmem((half * slab, LANES), F32),
        vmem((half * slab, LANES), BF16),
        vmem((NY - 1, NZ * slab, LANES), BF16),
        vmem((NZ * slab, LANES), F32),
        vmem((NZ * slab, LANES), BF16),
        vmem((NZ - 1, slab, LANES), BF16),
        vmem((slab, LANES), F32),
        vmem((nseq * SUB, LANES), F32),
        vmem((half * SUB, LANES), F32),
        vmem((half * SUB, LANES), F32),
        vmem((NY - 1, NZ * SUB, LANES), F32),
        vmem((NZ * SUB, LANES), F32),
        vmem((NZ - 1, SUB, LANES), F32),
        vmem((nseq * SUB, LANES), F32),
        vmem((nch, SUB, LANES), F32),
        vmem((NZ, SUB, LANES), F32),
        vmem((NY, SUB, LANES), F32),
        vmem((2, SUB, LANES), F32),
        pltpu.SemaphoreType.DMA((SEM_COUNT,)),
    ]
    gated, gproj, short, filt = pl.pallas_call(
        functools.partial(kernel, nseq, nch),
        name="hyena",
        out_shape=(
            jax.ShapeDtypeStruct((length, cols), BF16),
            jax.ShapeDtypeStruct((3, length, cols), BF16),
            jax.ShapeDtypeStruct((3, FK, cols), F32),
            jax.ShapeDtypeStruct((per_device, cols), F32),
        ),
        in_specs=[any_spec, any_spec] + [vmem_spec] * (3 + len(consts)),
        out_specs=(any_spec, any_spec, vmem_spec, vmem_spec),
        scratch_shapes=scratch,
        compiler_params=pltpu.CompilerParams(
            collective_id=0, has_side_effects=True, vmem_limit_bytes=64 * 1000 * 1000
        ),
    )(
        jnp.transpose(projected, (1, 0, 2)),
        cotangent,
        short_taps,
        filter_taps,
        decay.reshape(cbn, LANES),
        *consts,
    )
    return gated, jnp.transpose(gproj, (1, 0, 2)), short, filt


def solution(mesh):
    placed = (P("seq", None, "ch"), P(None, None, "ch"), P("seq", "ch"), P("ch"), P("seq", "ch"))
    nseq, nch = mesh.shape["seq"], mesh.shape["ch"]
    return jax.shard_map(
        functools.partial(shards, nseq, nch),
        mesh=mesh,
        in_specs=placed,
        out_specs=(P("seq", "ch"), P("seq", None, "ch"), P(None, None, "ch"), P("seq", "ch")),
        check_vma=False,
    )
```

```python
import functools
import math

import jax
import jax.numpy as jnp
import ml_dtypes
import numpy as np
from jax import lax
from jax.experimental import pallas as pl
from jax.experimental.pallas import tpu as pltpu
from jax.sharding import PartitionSpec as P

K = 128
FK = 7
HALO = FK - 1
NY = 4
NZ = 8
B = 128
N = 2 * B
W = 512
LANES = 128
SUB = 8
R = B // SUB
F32 = jnp.float32
BF16 = jnp.bfloat16
MESH = pl.DeviceIdType.MESH


def constants(per_device):
    place = np.arange(B)
    time = (place % SUB) * R + place // SUB
    order = np.zeros((B, B))
    order[place, time] = 1.0
    freq = np.concatenate([np.arange(0, B, 2), np.arange(1, B, 2)])
    sign = np.where(freq % 2 == 0, 1.0, -1.0)
    theta = 2.0 * np.pi * (freq + 0.5) / N
    slot = np.arange(K)
    end = slot % per_device
    rest = slot // per_device
    z, y, core = rest % NZ, (rest // NZ) % NY, rest // (NZ * NY)
    tap = ((y * NZ + z) * 2 + core) * per_device + end

    def forward(times):
        angle = theta[:, None] * times[None, :]
        full = np.concatenate([np.cos(angle), -np.sin(angle)], axis=0)
        high = full.astype(ml_dtypes.bfloat16)
        low = (full - high.astype(np.float64)).astype(ml_dtypes.bfloat16)
        return np.concatenate([high, low], axis=1)

    def inverse(times):
        angle = times[:, None] * theta[None, :]
        return np.concatenate([np.cos(angle), -np.sin(angle)], axis=1) * (2.0 / N)

    angle = tap[:, None] * theta[None, :]
    inv_corr = np.concatenate([np.sin(angle) * sign, np.cos(angle) * sign], axis=1) * (2.0 / N)
    as_bf16 = lambda value: np.asarray(value).astype(ml_dtypes.bfloat16)
    return tuple(
        as_bf16(value)
        for value in (
            order,
            order.T,
            forward(time),
            forward(tap),
            inverse(B + time),
            inverse(time),
            inv_corr,
        )
    )


def dot(a, b):
    return jnp.dot(a, b, preferred_element_type=F32)


def twice(value):
    return jnp.concatenate([value, value], axis=0)


def ahead(p, q):
    return [p[0] + q[2], p[1] - q[3], p[2] - q[0], p[3] + q[1]]


def short_conv(weights, full, back):
    total = None
    for j in range(FK):
        start = HALO - j if back else j
        term = weights[j] * full[start : start + R]
        total = term if total is None else total + term
    return total


def lag_sums(sums, grad, full):
    for j in range(FK):
        term = jnp.sum(grad * full[HALO - j : HALO - j + R], axis=0)
        sums[j] = term if sums[j] is None else sums[j] + term


class Sems:
    def __init__(self, ref):
        self.ref, self.used = ref, 0

    def take(self, count):
        first, self.used = self.used, self.used + count
        return first


SEM_COUNT = 256


def kernel(
    nseq,
    nch,
    proj,
    cot,
    short_taps,
    taps,
    decay,
    order_hbm,
    fwd_hbm,
    fwd_taps_hbm,
    inv_conv_hbm,
    inv_grad_hbm,
    inv_corr_hbm,
    gated_out,
    gproj_out,
    short_out,
    filter_out,
    xn,
    cn,
    xhalo,
    xp,
    feat,
    cotp,
    mx,
    gf,
    hx,
    hg,
    spec,
    hspec,
    prod,
    prod2,
    khat,
    kbf,
    kmine,
    kgather,
    kflat,
    conv,
    gfe,
    ghsend,
    ghrecv,
    og,
    op,
    fr,
    frc,
    fry_f,
    fry,
    fryr,
    frz_f,
    frz,
    frzr,
    frfin,
    sr,
    src_,
    sry,
    sryr,
    srz,
    srzr,
    ag,
    sqx,
    sqz,
    sqy,
    order,
    fwd,
    fwd_taps,
    inv_conv,
    inv_grad,
    inv_corr,
    sem_ref,
):
    consts_hbm = (order_hbm, fwd_hbm, inv_corr_hbm, fwd_taps_hbm, inv_conv_hbm, inv_grad_hbm)
    consts = (order, fwd, inv_corr, fwd_taps, inv_conv, inv_grad)
    cols = cot.shape[1]
    nchunk = cols // W
    cbn = cols // LANES
    per_device = taps.shape[0]
    slab = per_device * cbn
    half = NY * NZ
    me = lax.axis_index("seq")
    ch = lax.axis_index("ch")
    core = lax.rem(me, 2)
    z = lax.rem(me // 2, NZ)
    y = me // (2 * NZ)
    other = 1 - core
    seq_at = lambda yy, zz, cc: (yy * NZ + zz) * 2 + cc
    nxt = lax.rem(me + 1, nseq)
    prv = lax.rem(me + nseq - 1, nseq)
    at_z = [lax.rem(z + o, NZ) for o in range(NZ)]
    at_y = [lax.rem(y + o, NY) for o in range(NY)]
    at_x = [lax.rem(ch + o, nch) for o in range(nch)]
    from_z = [lax.rem(z + NZ - o, NZ) for o in range(NZ)]
    from_y = [lax.rem(y + NY - o, NY) for o in range(NY)]
    from_x = [lax.rem(ch + nch - o, nch) for o in range(nch)]
    dev_z = lambda o: (seq_at(y, at_z[o], core), ch)
    dev_y = lambda o: (seq_at(at_y[o], z, core), ch)
    dev_c = (seq_at(y, z, other), ch)
    dev_next, dev_prev = (nxt, ch), (prv, ch)
    sems = Sems(sem_ref)
    sends = []

    def remote(src, dst, send, recv, dev):
        return pltpu.make_async_remote_copy(
            src_ref=src,
            dst_ref=dst,
            send_sem=sem_ref.at[send],
            recv_sem=sem_ref.at[recv],
            device_id=dev,
            device_id_type=MESH,
        )

    def send(src, dst, ss, rs, dev):
        make = lambda: remote(src(), dst(), ss, rs, dev() if callable(dev) else dev)
        make().start()
        sends.append(make)

    def got(dst, ss, rs):
        remote(dst, dst, ss, rs, dev_next).wait_recv()

    s_in = sems.take(2 * nchunk)

    def load(c):
        at = pl.ds(pl.multiple_of(c * W, W), W)
        return (
            pltpu.make_async_copy(proj.at[:, :, at], xn.at[:, :, at], sem_ref.at[s_in + 2 * c]),
            pltpu.make_async_copy(cot.at[:, at], cn.at[:, at], sem_ref.at[s_in + 2 * c + 1]),
        )

    s_const = sems.take(len(consts_hbm))
    const_loads = [
        pltpu.make_async_copy(src, dst, sem_ref.at[s_const + k])
        for k, (src, dst) in enumerate(zip(consts_hbm, consts))
    ]
    for copy in const_loads[:2]:
        copy.start()
    for copy in load(0):
        copy.start()
    for copy in const_loads[2:]:
        copy.start()
    for c in range(1, nchunk):
        for copy in load(c):
            copy.start()

    barrier = pltpu.get_barrier_semaphore()
    near = [(o, dc) for o in range(nch) for dc in range(2) if o or dc]
    dev_near = lambda o, dc: (seq_at(y, z, lax.rem(core + dc, 2)), at_x[o])
    partners = [dev_next, dev_prev]
    partners += [dev_near(o, dc) for o, dc in near]
    partners += [dev_z(o) for o in range(1, NZ)]
    partners += [dev_y(o) for o in range(1, NY)]
    for dev in partners:
        pl.semaphore_signal(barrier, inc=1, device_id=dev, device_id_type=MESH)

    for e in range(per_device):
        lag = (me * per_device + e).astype(F32)
        fall = jnp.exp(-decay[...] * lag)
        for cb in range(cbn):
            row = taps[e : e + 1, cb * LANES : (cb + 1) * LANES]
            kflat[e * cbn + cb : e * cbn + cb + 1, :] = row
        part = pl.ds(e * cbn, cbn)
        kflat[part, :] = kflat[part, :] * fall
    slot = core * half + y * NZ + z
    slot_at = lambda cc, yy, zz: pl.ds(
        pl.multiple_of((cc * half + yy * NZ + zz) * slab, slab), slab
    )
    bundle_at = lambda cc, yy: pl.ds(
        pl.multiple_of((cc * half + yy * NZ) * slab, NZ * slab), NZ * slab
    )
    half_at = lambda cc: pl.ds(pl.multiple_of(cc * half * slab, half * slab), half * slab)
    kmine[...] = kflat[0:slab, :].astype(BF16)
    kgather[slot_at(core, y, z), :] = kmine[...]

    pl.semaphore_wait(barrier, len(partners))

    s_xh = sems.take(2)
    tail = proj.shape[1] - SUB
    send(lambda: proj.at[:, pl.ds(tail, SUB), :], lambda: xhalo, s_xh, s_xh + 1, dev_next)
    s_kz = sems.take(2 * NZ)
    own_slot = lambda: kgather.at[slot_at(core, y, z)]
    for o in range(1, NZ):
        send(lambda: kmine, own_slot, s_kz + o, s_kz + NZ + o, functools.partial(dev_z, o))
    s_ky = sems.take(2 * NY)
    s_kc = sems.take(2)
    for copy in const_loads:
        copy.wait()

    def taps_along_y():
        for o in range(1, NZ):
            got(kgather.at[slot_at(core, y, from_z[o])], s_kz + o, s_kz + NZ + o)
        own = lambda: kgather.at[bundle_at(core, y)]
        for o in range(1, NY):
            send(own, own, s_ky + o, s_ky + NY + o, functools.partial(dev_y, o))

    def taps_to_core():
        for o in range(1, NY):
            got(kgather.at[bundle_at(core, from_y[o])], s_ky + o, s_ky + NY + o)
        own = lambda: kgather.at[half_at(core)]
        send(own, own, s_kc, s_kc + 1, dev_c)

    first = jnp.where(me > 0, 1.0, 0.0).astype(F32)
    last = jnp.where(me < nseq - 1, 1.0, 0.0).astype(F32)
    row_id = lax.broadcasted_iota(jnp.int32, (HALO, SUB, LANES), 1)
    top, bottom = row_id == 0, row_id == SUB - 1
    rows = [slice(0, B), slice(B, 2 * B)]

    def tap_rows(i, at):
        return [jnp.broadcast_to(short_taps[i, j : j + 1, at], (SUB, LANES)) for j in range(FK)]

    s_hx = sems.take(2 * nchunk)
    s_hg = sems.take(2 * nchunk)

    def halo_x(c):
        at = pl.ds(pl.multiple_of(c * W, W), W)
        return remote(mx.at[pl.ds(B, B), at], hx.at[:, at], s_hx + c, s_hx + nchunk + c, dev_next)

    def halo_g(c):
        at = pl.ds(pl.multiple_of(c * W, W), W)
        return remote(gf.at[pl.ds(0, B), at], hg.at[:, at], s_hg + c, s_hg + nchunk + c, dev_prev)

    def features(c, carry):
        for copy in load(c):
            copy.wait()
        at = pl.ds(pl.multiple_of(c * W, W), W)
        for b in range(2):
            for i in range(3):
                xp[i, b, HALO:, :, at] = dot(order[...], xn[i, rows[b], at]).reshape(R, SUB, W)
            cotp[b, :, :, at] = dot(order[...], cn[rows[b], at]).reshape(R, SUB, W)

        @pl.when(c == 0)
        def _():
            got(xhalo, s_xh, s_xh + 1)

        @pl.when(c == min(2, nchunk - 1))
        def _():
            taps_along_y()

        def part_f(sub, inner):
            ls = pl.ds(pl.multiple_of(c * W + sub * LANES, LANES), LANES)
            feats = [[None] * 3, [None] * 3]
            for i in range(3):
                weights = tap_rows(i, ls)
                head = xhalo[i, :, ls].astype(F32) * first
                before = jnp.concatenate(
                    [
                        jnp.broadcast_to(head[2 + q : 3 + q, :], (SUB, LANES))[None]
                        for q in range(HALO)
                    ],
                    axis=0,
                )
                for b in range(2):
                    main = xp[i, b, HALO:, :, ls]
                    turned = pltpu.roll(main[R - HALO :], 1, axis=1)
                    early = jnp.where(top, before, turned)
                    before = turned
                    xp[i, b, :HALO, :, ls] = early
                    total = short_conv(weights, jnp.concatenate([early, main], axis=0), True)
                    feat[i, b, :, :, ls] = total
                    feats[b][i] = total
            for b in range(2):
                mixed = feats[b][1] * feats[b][2]
                mx[rows[b], ls] = mixed.reshape(B, LANES).astype(BF16)
                grad = cotp[b, :, :, ls] * feats[b][0]
                gf[rows[b], ls] = grad.reshape(B, LANES).astype(BF16)
            return inner

        lax.fori_loop(0, W // LANES, part_f, 0)
        halo_x(c).start()
        halo_g(c).start()
        for b in range(2):
            spec[b, :, at] = dot(fwd[...], twice(mx[rows[b], at]))
            spec[2 + b, :, at] = dot(fwd[...], twice(gf[rows[b], at]))
        return carry

    lax.fori_loop(0, nchunk, features, 0)

    quarter = B // 2

    def quads(ref, rs, ls):
        return [ref[pl.ds(q * quarter + rs, 32), ls] for q in range(4)]

    def correlate(c, carry):
        at = pl.ds(pl.multiple_of(c * W, W), W)
        halo_x(c).wait_recv()
        halo_g(c).wait_recv()
        hspec[0] = dot(fwd[...], twice(hx[:, at]))
        hspec[1] = dot(fwd[...], twice(hg[:, at]))
        def part_c(sub, inner):
            here = pl.ds(pl.multiple_of(sub * LANES, LANES), LANES)
            ls = pl.ds(pl.multiple_of(c * W + sub * LANES, LANES), LANES)
            for rs in range(0, quarter, 32):
                hq = [v * first for v in quads(hspec.at[0], rs, here)]
                gq = [v * last for v in quads(hspec.at[1], rs, here)]
                a, b, ga, gbq = [quads(spec.at[q], rs, ls) for q in range(4)]
                x0, x1 = ahead(hq, a), ahead(a, b)
                g0, g1 = ahead(ga, gbq), ahead(gbq, gq)
                for q in range(4):
                    part = pl.ds(q * quarter + rs, 32)
                    spec[0, part, ls] = x0[q]
                    spec[1, part, ls] = x1[q]
                    spec[2, part, ls] = g0[q]
                    spec[3, part, ls] = g1[q]
                for q in range(2):
                    re = ga[q] * x0[q] + ga[q + 2] * x0[q + 2]
                    re = re + (gbq[q] * x1[q] + gbq[q + 2] * x1[q + 2])
                    im = ga[q + 2] * x0[q] - ga[q] * x0[q + 2]
                    im = im + (gbq[q + 2] * x1[q] - gbq[q] * x1[q + 2])
                    prod[0, pl.ds(q * quarter + rs, 32), here] = re.astype(BF16)
                    prod[0, pl.ds((q + 2) * quarter + rs, 32), here] = im.astype(BF16)
            return inner

        lax.fori_loop(0, W // LANES, part_c, 0)

        @pl.when(c == nchunk // 2)
        def _():
            taps_to_core()

        corr = dot(inv_corr[...], prod[0])
        for sub in range(W // LANES):
            cb = c * (W // LANES) + sub
            fr[pl.ds(cb, K, stride=cbn), :] = corr[:, sub * LANES : (sub + 1) * LANES]
        return carry

    lax.fori_loop(0, nchunk, correlate, 0)

    s_fc = sems.take(2)
    send(lambda: fr.at[half_at(other)], lambda: frc, s_fc, s_fc + 1, dev_c)
    got(kgather.at[half_at(other)], s_kc, s_kc + 1)
    kflat[...] = kgather[...].astype(F32)
    s_fy = sems.take(2 * NY)
    s_fz = sems.take(2 * NZ)
    quart = NZ * slab
    quart_at = lambda yy: pl.ds(pl.multiple_of(yy * quart, quart), quart)
    slab_at = lambda zz: pl.ds(pl.multiple_of(zz * slab, slab), slab)

    def filter_along_y():
        got(frc, s_fc, s_fc + 1)
        fry_f[...] = fr[half_at(core), :] + frc[...]
        fry[...] = fry_f[...].astype(BF16)
        for o in range(1, NY):
            source = lambda o=o: fry.at[quart_at(at_y[o])]
            send(source, lambda o=o: fryr.at[o - 1], s_fy + o, s_fy + NY + o, functools.partial(dev_y, o))

    def filter_along_z():
        for o in range(1, NY):
            got(fryr.at[o - 1], s_fy + o, s_fy + NY + o)
        total = fry_f[quart_at(y), :]
        for o in range(1, NY):
            total = total + fryr[o - 1].astype(F32)
        frz_f[...] = total
        frz[...] = total.astype(BF16)
        for o in range(1, NZ):
            source = lambda o=o: frz.at[slab_at(at_z[o])]
            send(source, lambda o=o: frzr.at[o - 1], s_fz + o, s_fz + NZ + o, functools.partial(dev_z, o))

    s_og = sems.take(nchunk)

    def store_gated(c):
        at = pl.ds(pl.multiple_of(c * W, W), W)
        return pltpu.make_async_copy(og.at[:, at], gated_out.at[:, at], sem_ref.at[s_og + c])

    def filters(c, carry):
        at = pl.ds(pl.multiple_of(c * W, W), W)

        @pl.when(c == min(1, nchunk - 1))
        def _():
            filter_along_y()

        @pl.when(c == nchunk - 1)
        def _():
            filter_along_z()

        for sub in range(W // LANES):
            cb = c * (W // LANES) + sub
            here = slice(sub * LANES, (sub + 1) * LANES)
            kbf[:, here] = kflat[pl.ds(cb, K, stride=cbn), :].astype(BF16)
        khat[...] = dot(fwd_taps[...], twice(kbf[...]))
        def part_p(sub, inner):
            here = pl.ds(pl.multiple_of(sub * LANES, LANES), LANES)
            ls = pl.ds(pl.multiple_of(c * W + sub * LANES, LANES), LANES)
            for rs in range(0, B, 32):
                re, im = pl.ds(rs, 32), pl.ds(B + rs, 32)
                kr, ki = khat[re, here], khat[im, here]
                for b in range(2):
                    xr, xi = spec[b, re, ls], spec[b, im, ls]
                    prod[b, re, here] = (kr * xr - ki * xi).astype(BF16)
                    prod[b, im, here] = (kr * xi + ki * xr).astype(BF16)
                    xr, xi = spec[2 + b, re, ls], spec[2 + b, im, ls]
                    prod2[b, re, here] = (kr * xr + ki * xi).astype(BF16)
                    prod2[b, im, here] = (kr * xi - ki * xr).astype(BF16)
            return inner

        lax.fori_loop(0, W // LANES, part_p, 0)
        for b in range(2):
            conv[0, b] = dot(inv_conv[...], prod[b]).reshape(R, SUB, W)
            conv[1, b] = dot(inv_grad[...], prod2[b]).reshape(R, SUB, W)
        def part_g(sub, inner):
            here = pl.ds(pl.multiple_of(sub * LANES, LANES), LANES)
            ls = pl.ds(pl.multiple_of(c * W + sub * LANES, LANES), LANES)
            zero = jnp.zeros((1, LANES), F32)
            cb = c * (W // LANES) + sub
            sums = [[None] * FK for _ in range(3)]
            for b in range(2):
                filtered, mixed_grad = conv[0, b, :, :, here], conv[1, b, :, :, here]
                gate = feat[0, b, :, :, ls] * filtered
                og[rows[b], ls] = gate.reshape(B, LANES).astype(BF16)
                factors = [
                    (cotp[b, :, :, ls], filtered),
                    (mixed_grad, feat[2, b, :, :, ls]),
                    (mixed_grad, feat[1, b, :, :, ls]),
                ]
                for i, (one, two) in enumerate(factors):
                    grad = one * two
                    gfe[i, b, :, :, ls] = grad
                    lag_sums(sums[i], grad, xp[i, b, :, :, ls])
                    if b == 0:
                        heads = [grad[q, 0:1] for q in range(HALO)]
                        ghsend[i, :, ls] = jnp.concatenate(heads + [zero, zero], axis=0).astype(BF16)
            for i in range(3):
                parts = [jnp.sum(v, axis=0, keepdims=True) for v in sums[i]]
                at_slab = pl.ds(pl.multiple_of((i * cbn + cb) * SUB, SUB), SUB)
                sr[at_slab, :] = jnp.concatenate(parts + [zero], axis=0)
            return inner

        lax.fori_loop(0, W // LANES, part_g, 0)
        store_gated(c).start()
        return carry

    spare = nseq - 3 * cbn
    if spare > 0:
        sr[pl.ds(3 * cbn * SUB, spare * SUB), :] = jnp.zeros((spare * SUB, LANES), F32)

    lax.fori_loop(0, nchunk, filters, 0)

    s_sc = sems.take(2)
    shalf = half * SUB
    shalf_at = lambda cc: pl.ds(pl.multiple_of(cc * shalf, shalf), shalf)
    send(lambda: sr.at[shalf_at(other)], lambda: src_, s_sc, s_sc + 1, dev_c)
    s_gh = sems.take(2)
    send(lambda: ghsend, lambda: ghrecv, s_gh, s_gh + 1, dev_prev)
    s_sy = sems.take(2 * NY)
    sq_rows = NZ * SUB
    sq_at = lambda yy: pl.ds(pl.multiple_of(yy * sq_rows, sq_rows), sq_rows)
    got(src_, s_sc, s_sc + 1)
    sry[...] = sr[shalf_at(core), :] + src_[...]
    for o in range(1, NY):
        source = lambda o=o: sry.at[sq_at(at_y[o])]
        send(source, lambda o=o: sryr.at[o - 1], s_sy + o, s_sy + NY + o, functools.partial(dev_y, o))

    got(ghrecv, s_gh, s_gh + 1)
    s_op = sems.take(nchunk)

    def store_gproj(c):
        at = pl.ds(pl.multiple_of(c * W, W), W)
        return pltpu.make_async_copy(op.at[:, :, at], gproj_out.at[:, :, at], sem_ref.at[s_op + c])

    def backward(c, carry):
        at = pl.ds(pl.multiple_of(c * W, W), W)
        for i in range(3):
            def part_b(sub, inner, i=i):
                here = pl.ds(pl.multiple_of(sub * LANES, LANES), LANES)
                ls = pl.ds(pl.multiple_of(c * W + sub * LANES, LANES), LANES)
                weights = tap_rows(i, ls)
                foot = ghrecv[i, :, ls].astype(F32) * last
                after = jnp.concatenate(
                    [
                        jnp.broadcast_to(foot[q : q + 1, :], (SUB, LANES))[None]
                        for q in range(HALO)
                    ],
                    axis=0,
                )
                for b in (1, 0):
                    turned = pltpu.roll(gfe[i, b, :HALO, :, ls], SUB - 1, axis=1)
                    main = gfe[i, b, :, :, ls]
                    late = jnp.where(bottom, after, turned)
                    after = turned
                    total = short_conv(weights, jnp.concatenate([main, late], axis=0), False)
                    op[i, rows[b], ls] = total.reshape(B, LANES).astype(BF16)
                return inner

            lax.fori_loop(0, W // LANES, part_b, 0)
        store_gproj(c).start()
        return carry

    s_sz = sems.take(2 * NZ)
    s_az = sems.take(2 * NZ)
    s_ay = sems.take(2 * NY)
    s_ac = sems.take(2)
    s_qx = sems.take(4 * nch)
    s_qz = sems.take(2 * NZ)
    s_qy = sems.take(2 * NY)
    one_at = lambda zz: pl.ds(pl.multiple_of(zz * SUB, SUB), SUB)
    s_at = lambda cc, yy, zz: pl.ds(pl.multiple_of((cc * half + yy * NZ + zz) * SUB, SUB), SUB)
    s_bundle = lambda cc, yy: pl.ds(
        pl.multiple_of((cc * half + yy * NZ) * SUB, NZ * SUB), NZ * SUB
    )

    def shorts_along_z():
        for o in range(1, NY):
            got(sryr.at[o - 1], s_sy + o, s_sy + NY + o)
        total = sry[sq_at(y), :]
        for o in range(1, NY):
            total = total + sryr[o - 1]
        srz[...] = total
        for o in range(1, NZ):
            source = lambda o=o: srz.at[one_at(at_z[o])]
            send(source, lambda o=o: srzr.at[o - 1], s_sz + o, s_sz + NZ + o, functools.partial(dev_z, o))

    def sums_done():
        for o in range(1, NZ):
            got(srzr.at[o - 1], s_sz + o, s_sz + NZ + o)
        mine = srz[one_at(z), :]
        for o in range(1, NZ):
            mine = mine + srzr[o - 1]
        ag[s_at(core, y, z), :] = mine
        own = lambda: ag.at[s_at(core, y, z)]
        for o in range(1, NZ):
            send(own, own, s_az + o, s_az + NZ + o, functools.partial(dev_z, o))
        for o in range(1, NZ):
            got(frzr.at[o - 1], s_fz + o, s_fz + NZ + o)
        total = frz_f[slab_at(z), :]
        for o in range(1, NZ):
            total = total + frzr[o - 1].astype(F32)
        square = mine * mine
        for e in range(per_device):
            lag = (me * per_device + e).astype(F32)
            value = total[e * cbn : (e + 1) * cbn, :] * jnp.exp(-decay[...] * lag)
            frfin[pl.ds(e * cbn, cbn), :] = value
        whole = frfin[...]
        square = square + jnp.sum((whole * whole).reshape(slab // SUB, SUB, LANES), axis=0)
        spot = ch * 2 + core
        sqx[spot] = square
        for o, dc in near:
            base = s_qx + o * 2 + dc
            place = lambda: sqx.at[spot]
            send(place, place, base, base + 2 * nch, functools.partial(dev_near, o, dc))

    lax.fori_loop(0, nchunk // 2, backward, 0)
    shorts_along_z()
    lax.fori_loop(nchunk // 2, nchunk, backward, 0)
    sums_done()

    def added(buf, count):
        value = buf[0]
        for k in range(1, count):
            value = value + buf[k]
        return value

    def share(buf, value, spot, base, count, to):
        buf[spot] = value
        place = lambda: buf.at[spot]
        for o in range(1, count):
            send(place, place, base + o, base + count + o, functools.partial(to, o))

    for o, dc in near:
        base = s_qx + o * 2 + dc
        place = from_x[o] * 2 + lax.rem(core + dc, 2)
        got(sqx.at[place], base, base + 2 * nch)
    share(sqz, added(sqx, 2 * nch), z, s_qz, NZ, dev_z)

    for o in range(1, NZ):
        got(ag.at[s_at(core, y, from_z[o])], s_az + o, s_az + NZ + o)
    own_bundle = lambda: ag.at[s_bundle(core, y)]
    for o in range(1, NY):
        send(own_bundle, own_bundle, s_ay + o, s_ay + NY + o, functools.partial(dev_y, o))

    for o in range(1, NZ):
        got(sqz.at[from_z[o]], s_qz + o, s_qz + NZ + o)
    share(sqy, added(sqz, NZ), y, s_qy, NY, dev_y)

    for o in range(1, NY):
        got(ag.at[s_bundle(core, from_y[o])], s_ay + o, s_ay + NY + o)
    own_half = lambda: ag.at[shalf_at(core)]
    send(own_half, own_half, s_ac, s_ac + 1, dev_c)

    for o in range(1, NY):
        got(sqy.at[from_y[o]], s_qy + o, s_qy + NY + o)
    square = added(sqy, NY)
    sums = jnp.sum(jnp.sum(square, axis=0, keepdims=True), axis=1, keepdims=True)
    channels = cols * nch
    limit = math.sqrt(K * channels + 3 * FK * channels)
    scale = jnp.minimum(1.0, limit / jnp.sqrt(sums))
    for e in range(per_device):
        for cb in range(cbn):
            value = frfin[e * cbn + cb : e * cbn + cb + 1, :] * scale
            filter_out[e : e + 1, cb * LANES : (cb + 1) * LANES] = value
    got(ag.at[shalf_at(other)], s_ac, s_ac + 1)
    for i in range(3):
        for cb in range(cbn):
            first_row = (i * cbn + cb) * SUB
            value = ag[first_row : first_row + FK, :] * scale
            short_out[i, :, cb * LANES : (cb + 1) * LANES] = value

    def finish(c, carry):
        halo_x(c).wait_send()
        halo_g(c).wait_send()
        store_gated(c).wait()
        store_gproj(c).wait()
        return carry

    lax.fori_loop(0, nchunk, finish, 0)
    for make in sends:
        make().wait_send()


def restore(order_t, gated, gproj, short, filt, gated_out, gproj_out, short_out, filt_out):
    for b in range(2):
        rows = slice(b * B, (b + 1) * B)
        gated_out[rows, :] = dot(order_t[...], gated[rows, :]).astype(BF16)
        for i in range(3):
            gproj_out[i, rows, :] = dot(order_t[...], gproj[i, rows, :]).astype(BF16)

    @pl.when(pl.program_id(0) == 0)
    def _():
        short_out[...] = short[...]
        filt_out[...] = filt[...]


def shards(nseq, nch, projected, short_taps, filter_taps, decay, cotangent):
    length, cols = cotangent.shape
    per_device = filter_taps.shape[0]
    cbn = cols // LANES
    slab = per_device * cbn
    half = NY * NZ
    nchunk = cols // W
    vmem = pltpu.VMEM
    order, order_t, *rest = [jnp.asarray(value) for value in constants(per_device)]
    consts = [order, *rest]
    any_spec = pl.BlockSpec(memory_space=pl.ANY)
    vmem_spec = pl.BlockSpec(memory_space=pltpu.VMEM)
    scratch = [
        vmem((3, length, cols), BF16),
        vmem((length, cols), BF16),
        vmem((3, SUB, cols), BF16),
        vmem((3, 2, R + HALO, SUB, cols), F32),
        vmem((3, 2, R, SUB, cols), F32),
        vmem((2, R, SUB, cols), F32),
        vmem((length, cols), BF16),
        vmem((length, cols), BF16),
        vmem((B, cols), BF16),
        vmem((B, cols), BF16),
        vmem((4, N, cols), F32),
        vmem((2, N, W), F32),
        vmem((2, N, W), BF16),
        vmem((2, N, W), BF16),
        vmem((N, W), F32),
        vmem((K, W), BF16),
        vmem((slab, LANES), BF16),
        vmem((K * cbn, LANES), BF16),
        vmem((K * cbn, LANES), F32),
        vmem((2, 2, R, SUB, W), F32),
        vmem((3, 2, R, SUB, cols), F32),
        vmem((3, SUB, cols), BF16),
        vmem((3, SUB, cols), BF16),
        vmem((length, cols), BF16),
        vmem((3, length, cols), BF16),
        vmem((K * cbn, LANES), F32),
        vmem((half * slab, LANES), F32),
        vmem((half * slab, LANES), F32),
        vmem((half * slab, LANES), BF16),
        vmem((NY - 1, NZ * slab, LANES), BF16),
        vmem((NZ * slab, LANES), F32),
        vmem((NZ * slab, LANES), BF16),
        vmem((NZ - 1, slab, LANES), BF16),
        vmem((slab, LANES), F32),
        vmem((nseq * SUB, LANES), F32),
        vmem((half * SUB, LANES), F32),
        vmem((half * SUB, LANES), F32),
        vmem((NY - 1, NZ * SUB, LANES), F32),
        vmem((NZ * SUB, LANES), F32),
        vmem((NZ - 1, SUB, LANES), F32),
        vmem((nseq * SUB, LANES), F32),
        vmem((2 * nch, SUB, LANES), F32),
        vmem((NZ, SUB, LANES), F32),
        vmem((NY, SUB, LANES), F32),
        vmem((B, B), BF16),
        vmem((N, N), BF16),
        vmem((N, N), BF16),
        vmem((B, N), BF16),
        vmem((B, N), BF16),
        vmem((B, N), BF16),
        pltpu.SemaphoreType.DMA((SEM_COUNT,)),
    ]
    gated, gproj, short, filt = pl.pallas_call(
        functools.partial(kernel, nseq, nch),
        name="hyena",
        out_shape=(
            jax.ShapeDtypeStruct((length, cols), BF16),
            jax.ShapeDtypeStruct((3, length, cols), BF16),
            jax.ShapeDtypeStruct((3, FK, cols), F32),
            jax.ShapeDtypeStruct((per_device, cols), F32),
        ),
        in_specs=[any_spec, any_spec] + [vmem_spec] * 3 + [any_spec] * len(consts),
        out_specs=(any_spec, any_spec, vmem_spec, vmem_spec),
        scratch_shapes=scratch,
        compiler_params=pltpu.CompilerParams(
            collective_id=0, has_side_effects=True, vmem_limit_bytes=64 * 1000 * 1000
        ),
    )(
        jnp.transpose(projected, (1, 0, 2)),
        cotangent,
        short_taps,
        filter_taps,
        decay.reshape(cbn, LANES),
        *consts,
    )
    wide = min(512, cols)
    flat = pl.BlockSpec((length, wide), lambda c: (0, c))
    deep = pl.BlockSpec((3, length, wide), lambda c: (0, 0, c))
    whole = lambda array: pl.BlockSpec(array.shape, lambda c: (0,) * array.ndim)
    gated, gproj, short, filt = pl.pallas_call(
        restore,
        name="restore",
        grid=(cols // wide,),
        out_shape=tuple(
            jax.ShapeDtypeStruct(array.shape, array.dtype) for array in (gated, gproj, short, filt)
        ),
        in_specs=[whole(order_t), flat, deep, whole(short), whole(filt)],
        out_specs=(flat, deep, whole(short), whole(filt)),
    )(order_t, gated, gproj, short, filt)
    return gated, jnp.transpose(gproj, (1, 0, 2)), short, filt


def solution(mesh):
    placed = (P("seq", None, "ch"), P(None, None, "ch"), P("seq", "ch"), P("ch"), P("seq", "ch"))
    nseq, nch = mesh.shape["seq"], mesh.shape["ch"]
    return jax.shard_map(
        functools.partial(shards, nseq, nch),
        mesh=mesh,
        in_specs=placed,
        out_specs=(P("seq", "ch"), P("seq", None, "ch"), P(None, None, "ch"), P("seq", "ch")),
        check_vma=False,
    )
```

```python
import functools
import math

import jax
import jax.numpy as jnp
import ml_dtypes
import numpy as np
from jax import lax
from jax.experimental import pallas as pl
from jax.experimental.pallas import tpu as pltpu
from jax.sharding import PartitionSpec as P

K = 128
FK = 7
HALO = FK - 1
NY = 4
NZ = 8
B = 128
N = 2 * B
W = 512
LANES = 128
SUB = 8
R = B // SUB
F32 = jnp.float32
BF16 = jnp.bfloat16
MESH = pl.DeviceIdType.MESH


def constants(per_device):
    place = np.arange(B)
    time = (place % SUB) * R + place // SUB
    order = np.zeros((B, B))
    order[place, time] = 1.0
    freq = np.concatenate([np.arange(0, B, 2), np.arange(1, B, 2)])
    sign = np.where(freq % 2 == 0, 1.0, -1.0)
    theta = 2.0 * np.pi * (freq + 0.5) / N
    slot = np.arange(K)
    end = slot % per_device
    rest = slot // per_device
    z, y, core = rest % NZ, (rest // NZ) % NY, rest // (NZ * NY)
    tap = ((y * NZ + z) * 2 + core) * per_device + end

    def forward(times):
        angle = theta[:, None] * times[None, :]
        full = np.concatenate([np.cos(angle), -np.sin(angle)], axis=0)
        high = full.astype(ml_dtypes.bfloat16)
        low = (full - high.astype(np.float64)).astype(ml_dtypes.bfloat16)
        return np.concatenate([high, low], axis=1)

    def inverse(times):
        angle = times[:, None] * theta[None, :]
        return np.concatenate([np.cos(angle), -np.sin(angle)], axis=1) * (2.0 / N)

    angle = tap[:, None] * theta[None, :]
    inv_corr = np.concatenate([np.sin(angle) * sign, np.cos(angle) * sign], axis=1) * (2.0 / N)
    as_bf16 = lambda value: np.asarray(value).astype(ml_dtypes.bfloat16)
    return tuple(
        as_bf16(value)
        for value in (
            order,
            order.T,
            forward(time),
            forward(tap),
            inverse(B + time),
            inverse(time),
            inv_corr,
        )
    )


def dot(a, b):
    return jnp.dot(a, b, preferred_element_type=F32)


def twice(value):
    return jnp.concatenate([value, value], axis=0)


def ahead(p, q):
    return [p[0] + q[2], p[1] - q[3], p[2] - q[0], p[3] + q[1]]


def short_conv(weights, full, back):
    total = None
    for j in range(FK):
        start = HALO - j if back else j
        term = weights[j] * full[start : start + R]
        total = term if total is None else total + term
    return total


def lag_sums(sums, grad, full):
    for j in range(FK):
        term = jnp.sum(grad * full[HALO - j : HALO - j + R], axis=0)
        sums[j] = term if sums[j] is None else sums[j] + term


class Sems:
    def __init__(self, ref):
        self.ref, self.used = ref, 0

    def take(self, count):
        first, self.used = self.used, self.used + count
        return first


SEM_COUNT = 256


def kernel(
    nseq,
    nch,
    proj,
    cot,
    short_taps,
    taps,
    decay,
    order_hbm,
    fwd_hbm,
    fwd_taps_hbm,
    inv_conv_hbm,
    inv_grad_hbm,
    inv_corr_hbm,
    gated_out,
    gproj_out,
    short_out,
    filter_out,
    xn,
    cn,
    xhalo,
    xp,
    feat,
    cotp,
    mx,
    gf,
    hx,
    hg,
    spec,
    hspec,
    prod,
    prod2,
    khat,
    kbf,
    kmine,
    kgather,
    kflat,
    conv,
    gfe,
    ghsend,
    ghrecv,
    og,
    op,
    fr,
    frs,
    frc,
    fry_f,
    fry,
    fryr,
    frz_f,
    frz,
    frzr,
    frfin,
    sr,
    src_,
    srf,
    srb,
    srzr,
    sryr,
    ag,
    sqx,
    sqz,
    sqy,
    order,
    fwd,
    fwd_taps,
    inv_conv,
    inv_grad,
    inv_corr,
    sem_ref,
):
    consts_hbm = (order_hbm, fwd_hbm, inv_corr_hbm, fwd_taps_hbm, inv_conv_hbm, inv_grad_hbm)
    consts = (order, fwd, inv_corr, fwd_taps, inv_conv, inv_grad)
    cols = cot.shape[1]
    nchunk = cols // W
    cbn = cols // LANES
    per_device = taps.shape[0]
    slab = per_device * cbn
    half = NY * NZ
    me = lax.axis_index("seq")
    ch = lax.axis_index("ch")
    core = lax.rem(me, 2)
    z = lax.rem(me // 2, NZ)
    y = me // (2 * NZ)
    other = 1 - core
    seq_at = lambda yy, zz, cc: (yy * NZ + zz) * 2 + cc
    nxt = lax.rem(me + 1, nseq)
    prv = lax.rem(me + nseq - 1, nseq)
    at_z = [lax.rem(z + o, NZ) for o in range(NZ)]
    at_y = [lax.rem(y + o, NY) for o in range(NY)]
    at_x = [lax.rem(ch + o, nch) for o in range(nch)]
    from_z = [lax.rem(z + NZ - o, NZ) for o in range(NZ)]
    from_y = [lax.rem(y + NY - o, NY) for o in range(NY)]
    from_x = [lax.rem(ch + nch - o, nch) for o in range(nch)]
    dev_z = lambda o: (seq_at(y, at_z[o], core), ch)
    dev_y = lambda o: (seq_at(at_y[o], z, core), ch)
    dev_c = (seq_at(y, z, other), ch)
    dev_next, dev_prev = (nxt, ch), (prv, ch)
    sems = Sems(sem_ref)
    sends = []

    def remote(src, dst, send, recv, dev):
        return pltpu.make_async_remote_copy(
            src_ref=src,
            dst_ref=dst,
            send_sem=sem_ref.at[send],
            recv_sem=sem_ref.at[recv],
            device_id=dev,
            device_id_type=MESH,
        )

    def send(src, dst, ss, rs, dev):
        make = lambda: remote(src(), dst(), ss, rs, dev() if callable(dev) else dev)
        make().start()
        sends.append(make)

    def got(dst, ss, rs):
        remote(dst, dst, ss, rs, dev_next).wait_recv()

    s_in = sems.take(2 * nchunk)

    def load(c):
        at = pl.ds(pl.multiple_of(c * W, W), W)
        return (
            pltpu.make_async_copy(proj.at[:, :, at], xn.at[:, :, at], sem_ref.at[s_in + 2 * c]),
            pltpu.make_async_copy(cot.at[:, at], cn.at[:, at], sem_ref.at[s_in + 2 * c + 1]),
        )

    s_const = sems.take(len(consts_hbm))
    const_loads = [
        pltpu.make_async_copy(src, dst, sem_ref.at[s_const + k])
        for k, (src, dst) in enumerate(zip(consts_hbm, consts))
    ]
    for copy in const_loads[:2]:
        copy.start()
    for copy in load(0):
        copy.start()
    for copy in const_loads[2:]:
        copy.start()
    for c in range(1, nchunk):
        for copy in load(c):
            copy.start()

    barrier = pltpu.get_barrier_semaphore()
    near = [(o, dc) for o in range(nch) for dc in range(2) if o or dc]
    dev_near = lambda o, dc: (seq_at(y, z, lax.rem(core + dc, 2)), at_x[o])
    partners = [dev_next, dev_prev]
    partners += [dev_near(o, dc) for o, dc in near]
    partners += [dev_z(o) for o in range(1, NZ)]
    partners += [dev_y(o) for o in range(1, NY)]
    for dev in partners:
        pl.semaphore_signal(barrier, inc=1, device_id=dev, device_id_type=MESH)

    for e in range(per_device):
        lag = (me * per_device + e).astype(F32)
        fall = jnp.exp(-decay[...] * lag)
        for cb in range(cbn):
            row = taps[e : e + 1, cb * LANES : (cb + 1) * LANES]
            kflat[e * cbn + cb : e * cbn + cb + 1, :] = row
        part = pl.ds(e * cbn, cbn)
        kflat[part, :] = kflat[part, :] * fall
    slot = core * half + y * NZ + z
    slot_at = lambda cc, yy, zz: pl.ds(
        pl.multiple_of((cc * half + yy * NZ + zz) * slab, slab), slab
    )
    bundle_at = lambda cc, yy: pl.ds(
        pl.multiple_of((cc * half + yy * NZ) * slab, NZ * slab), NZ * slab
    )
    half_at = lambda cc: pl.ds(pl.multiple_of(cc * half * slab, half * slab), half * slab)
    kmine[...] = kflat[0:slab, :].astype(BF16)
    kgather[slot_at(core, y, z), :] = kmine[...]

    rows = [slice(0, B), slice(B, 2 * B)]
    const_loads[0].wait()

    def reorder(c, carry):
        for copy in load(c):
            copy.wait()
        at = pl.ds(pl.multiple_of(c * W, W), W)
        for b in range(2):
            for i in range(3):
                xp[i, b, HALO:, :, at] = dot(order[...], xn[i, rows[b], at]).reshape(R, SUB, W)
            cotp[b, :, :, at] = dot(order[...], cn[rows[b], at]).reshape(R, SUB, W)
        return carry

    lax.fori_loop(0, nchunk, reorder, 0)

    pl.semaphore_wait(barrier, len(partners))

    s_xh = sems.take(2)
    tail = proj.shape[1] - SUB
    send(lambda: proj.at[:, pl.ds(tail, SUB), :], lambda: xhalo, s_xh, s_xh + 1, dev_next)
    s_kz = sems.take(2 * NZ)
    own_slot = lambda: kgather.at[slot_at(core, y, z)]
    for o in range(1, NZ):
        send(lambda: kmine, own_slot, s_kz + o, s_kz + NZ + o, functools.partial(dev_z, o))
    s_ky = sems.take(2 * NY)
    s_kc = sems.take(2)
    for copy in const_loads[1:]:
        copy.wait()

    def taps_along_y():
        for o in range(1, NZ):
            got(kgather.at[slot_at(core, y, from_z[o])], s_kz + o, s_kz + NZ + o)
        own = lambda: kgather.at[bundle_at(core, y)]
        for o in range(1, NY):
            send(own, own, s_ky + o, s_ky + NY + o, functools.partial(dev_y, o))

    def taps_to_core():
        for o in range(1, NY):
            got(kgather.at[bundle_at(core, from_y[o])], s_ky + o, s_ky + NY + o)
        own = lambda: kgather.at[half_at(core)]
        send(own, own, s_kc, s_kc + 1, dev_c)

    first = jnp.where(me > 0, 1.0, 0.0).astype(F32)
    last = jnp.where(me < nseq - 1, 1.0, 0.0).astype(F32)
    row_id = lax.broadcasted_iota(jnp.int32, (HALO, SUB, LANES), 1)
    top, bottom = row_id == 0, row_id == SUB - 1

    def tap_rows(i, at):
        return [jnp.broadcast_to(short_taps[i, j : j + 1, at], (SUB, LANES)) for j in range(FK)]

    s_hx = sems.take(2 * nchunk)
    s_hg = sems.take(2 * nchunk)

    def halo_x(c):
        at = pl.ds(pl.multiple_of(c * W, W), W)
        return remote(mx.at[pl.ds(B, B), at], hx.at[:, at], s_hx + c, s_hx + nchunk + c, dev_next)

    def halo_g(c):
        at = pl.ds(pl.multiple_of(c * W, W), W)
        return remote(gf.at[pl.ds(0, B), at], hg.at[:, at], s_hg + c, s_hg + nchunk + c, dev_prev)

    def features(b, c, carry):
        at = pl.ds(pl.multiple_of(c * W, W), W)
        if b == 0:

            @pl.when(c == nchunk // 2)
            def _():
                taps_along_y()

        def one(sub, inner):
            ls = pl.ds(pl.multiple_of(c * W + sub * LANES, LANES), LANES)
            feats = []
            for i in range(3):
                weights = tap_rows(i, ls)
                if b == 0:
                    head = xhalo[i, :, ls].astype(F32) * first
                    before = jnp.concatenate(
                        [
                            jnp.broadcast_to(head[2 + q : 3 + q, :], (SUB, LANES))[None]
                            for q in range(HALO)
                        ],
                        axis=0,
                    )
                else:
                    before = pltpu.roll(xp[i, 0, R:, :, ls], 1, axis=1)
                main = xp[i, b, HALO:, :, ls]
                turned = pltpu.roll(main[R - HALO :], 1, axis=1)
                early = jnp.where(top, before, turned)
                xp[i, b, :HALO, :, ls] = early
                total = short_conv(weights, jnp.concatenate([early, main], axis=0), True)
                feat[i, b, :, :, ls] = total
                feats.append(total)
            mx[rows[b], ls] = (feats[1] * feats[2]).reshape(B, LANES).astype(BF16)
            gf[rows[b], ls] = (cotp[b, :, :, ls] * feats[0]).reshape(B, LANES).astype(BF16)
            return inner

        lax.fori_loop(0, W // LANES, one, 0)
        if b == 0:
            halo_g(c).start()
        else:
            halo_x(c).start()
        spec[b, :, at] = dot(fwd[...], twice(mx[rows[b], at]))
        spec[2 + b, :, at] = dot(fwd[...], twice(gf[rows[b], at]))
        return carry

    lax.fori_loop(0, nchunk, functools.partial(features, 1), 0)
    got(xhalo, s_xh, s_xh + 1)
    lax.fori_loop(0, nchunk, functools.partial(features, 0), 0)

    quarter = B // 2

    def quads(ref, rs, ls):
        return [ref[pl.ds(q * quarter + rs, 16), ls] for q in range(4)]

    def correlate(c, carry):
        at = pl.ds(pl.multiple_of(c * W, W), W)
        halo_x(c).wait_recv()
        halo_g(c).wait_recv()
        hspec[0] = dot(fwd[...], twice(hx[:, at]))
        hspec[1] = dot(fwd[...], twice(hg[:, at]))
        def part_c(sub, inner):
            here = pl.ds(pl.multiple_of(sub * LANES, LANES), LANES)
            ls = pl.ds(pl.multiple_of(c * W + sub * LANES, LANES), LANES)
            for rs in range(0, quarter, 16):
                hq = [v * first for v in quads(hspec.at[0], rs, here)]
                gq = [v * last for v in quads(hspec.at[1], rs, here)]
                a, b, ga, gbq = [quads(spec.at[q], rs, ls) for q in range(4)]
                x0, x1 = ahead(hq, a), ahead(a, b)
                g0, g1 = ahead(ga, gbq), ahead(gbq, gq)
                for q in range(4):
                    part = pl.ds(q * quarter + rs, 16)
                    spec[0, part, ls] = x0[q]
                    spec[1, part, ls] = x1[q]
                    spec[2, part, ls] = g0[q]
                    spec[3, part, ls] = g1[q]
                for q in range(2):
                    re = ga[q] * x0[q] + ga[q + 2] * x0[q + 2]
                    re = re + (gbq[q] * x1[q] + gbq[q + 2] * x1[q + 2])
                    im = ga[q + 2] * x0[q] - ga[q] * x0[q + 2]
                    im = im + (gbq[q + 2] * x1[q] - gbq[q] * x1[q + 2])
                    prod[0, pl.ds(q * quarter + rs, 16), here] = re.astype(BF16)
                    prod[0, pl.ds((q + 2) * quarter + rs, 16), here] = im.astype(BF16)
            return inner

        lax.fori_loop(0, W // LANES, part_c, 0)

        @pl.when(c == nchunk - 1)
        def _():
            taps_to_core()

        corr = dot(inv_corr[...], prod[0])
        for sub in range(W // LANES):
            cb = c * (W // LANES) + sub
            fr[pl.ds(cb, K, stride=cbn), :] = corr[:, sub * LANES : (sub + 1) * LANES]
        return carry

    lax.fori_loop(0, nchunk, correlate, 0)

    s_fc = sems.take(2)
    frs[...] = fr[half_at(other), :].astype(BF16)
    send(lambda: frs, lambda: frc, s_fc, s_fc + 1, dev_c)
    got(kgather.at[half_at(other)], s_kc, s_kc + 1)
    kflat[...] = kgather[...].astype(F32)
    s_fy = sems.take(2 * NY)
    s_fz = sems.take(2 * NZ)
    quart = NZ * slab
    quart_at = lambda yy: pl.ds(pl.multiple_of(yy * quart, quart), quart)
    slab_at = lambda zz: pl.ds(pl.multiple_of(zz * slab, slab), slab)

    def filter_along_y():
        got(frc, s_fc, s_fc + 1)
        fry_f[...] = fr[half_at(core), :] + frc[...].astype(F32)
        fry[...] = fry_f[...].astype(BF16)
        for o in range(1, NY):
            source = lambda o=o: fry.at[quart_at(at_y[o])]
            send(source, lambda o=o: fryr.at[o - 1], s_fy + o, s_fy + NY + o, functools.partial(dev_y, o))

    def filter_along_z():
        for o in range(1, NY):
            got(fryr.at[o - 1], s_fy + o, s_fy + NY + o)
        total = fry_f[quart_at(y), :]
        for o in range(1, NY):
            total = total + fryr[o - 1].astype(F32)
        frz_f[...] = total
        frz[...] = total.astype(BF16)
        for o in range(1, NZ):
            source = lambda o=o: frz.at[slab_at(at_z[o])]
            send(source, lambda o=o: frzr.at[o - 1], s_fz + o, s_fz + NZ + o, functools.partial(dev_z, o))

    s_og = sems.take(nchunk)

    def store_gated(c):
        at = pl.ds(pl.multiple_of(c * W, W), W)
        return pltpu.make_async_copy(og.at[:, at], gated_out.at[:, at], sem_ref.at[s_og + c])

    def filters(c, carry):
        at = pl.ds(pl.multiple_of(c * W, W), W)

        @pl.when(c == min(1, nchunk - 1))
        def _():
            filter_along_y()

        for sub in range(W // LANES):
            cb = c * (W // LANES) + sub
            here = slice(sub * LANES, (sub + 1) * LANES)
            kbf[:, here] = kflat[pl.ds(cb, K, stride=cbn), :].astype(BF16)
        khat[...] = dot(fwd_taps[...], twice(kbf[...]))
        def part_p(sub, inner):
            here = pl.ds(pl.multiple_of(sub * LANES, LANES), LANES)
            ls = pl.ds(pl.multiple_of(c * W + sub * LANES, LANES), LANES)
            for rs in range(0, B, 16):
                re, im = pl.ds(rs, 16), pl.ds(B + rs, 16)
                kr, ki = khat[re, here], khat[im, here]
                for b in range(2):
                    xr, xi = spec[b, re, ls], spec[b, im, ls]
                    prod[b, re, here] = (kr * xr - ki * xi).astype(BF16)
                    prod[b, im, here] = (kr * xi + ki * xr).astype(BF16)
                    xr, xi = spec[2 + b, re, ls], spec[2 + b, im, ls]
                    prod2[b, re, here] = (kr * xr + ki * xi).astype(BF16)
                    prod2[b, im, here] = (kr * xi - ki * xr).astype(BF16)
            return inner

        lax.fori_loop(0, W // LANES, part_p, 0)
        for b in range(2):
            conv[0, b] = dot(inv_conv[...], prod[b]).reshape(R, SUB, W)
            conv[1, b] = dot(inv_grad[...], prod2[b]).reshape(R, SUB, W)
        def part_g(sub, inner):
            here = pl.ds(pl.multiple_of(sub * LANES, LANES), LANES)
            ls = pl.ds(pl.multiple_of(c * W + sub * LANES, LANES), LANES)
            zero = jnp.zeros((1, LANES), F32)
            cb = c * (W // LANES) + sub
            sums = [[None] * FK for _ in range(3)]
            for b in range(2):
                filtered, mixed_grad = conv[0, b, :, :, here], conv[1, b, :, :, here]
                gate = feat[0, b, :, :, ls] * filtered
                og[rows[b], ls] = gate.reshape(B, LANES).astype(BF16)
                factors = [
                    (cotp[b, :, :, ls], filtered),
                    (mixed_grad, feat[2, b, :, :, ls]),
                    (mixed_grad, feat[1, b, :, :, ls]),
                ]
                for i, (one, two) in enumerate(factors):
                    grad = one * two
                    gfe[i, b, :, :, ls] = grad
                    lag_sums(sums[i], grad, xp[i, b, :, :, ls])
                    if b == 0:
                        heads = [grad[q, 0:1] for q in range(HALO)]
                        ghsend[i, :, ls] = jnp.concatenate(heads + [zero, zero], axis=0).astype(BF16)
            for i in range(3):
                parts = [jnp.sum(v, axis=0, keepdims=True) for v in sums[i]]
                at_slab = pl.ds(pl.multiple_of((i * cbn + cb) * SUB, SUB), SUB)
                sr[at_slab, :] = jnp.concatenate(parts + [zero], axis=0)
            return inner

        lax.fori_loop(0, W // LANES, part_g, 0)
        store_gated(c).start()
        return carry

    lax.fori_loop(0, nchunk, filters, 0)

    s_sc = sems.take(2)
    shalf = 3 * cbn // 2 * SUB
    piece = shalf // NZ
    shalf_at = lambda cc: pl.ds(pl.multiple_of(cc * shalf, shalf), shalf)
    send(lambda: sr.at[shalf_at(other)], lambda: src_, s_sc, s_sc + 1, dev_c)
    s_gh = sems.take(2)
    send(lambda: ghsend, lambda: ghrecv, s_gh, s_gh + 1, dev_prev)
    s_sz = sems.take(2 * NZ)
    filter_along_z()
    got(src_, s_sc, s_sc + 1)
    srf[...] = (sr[shalf_at(core), :] + src_[...]).reshape(NZ, piece, LANES)
    srb[...] = srf[...].astype(BF16)
    for o in range(1, NZ):
        source = lambda o=o: srb.at[at_z[o]]
        send(source, lambda: srzr.at[z], s_sz + o, s_sz + NZ + o, functools.partial(dev_z, o))

    got(ghrecv, s_gh, s_gh + 1)
    s_op = sems.take(nchunk)

    def store_gproj(c):
        at = pl.ds(pl.multiple_of(c * W, W), W)
        return pltpu.make_async_copy(op.at[:, :, at], gproj_out.at[:, :, at], sem_ref.at[s_op + c])

    def backward(c, carry):
        at = pl.ds(pl.multiple_of(c * W, W), W)
        for i in range(3):
            def part_b(sub, inner, i=i):
                here = pl.ds(pl.multiple_of(sub * LANES, LANES), LANES)
                ls = pl.ds(pl.multiple_of(c * W + sub * LANES, LANES), LANES)
                weights = tap_rows(i, ls)
                foot = ghrecv[i, :, ls].astype(F32) * last
                after = jnp.concatenate(
                    [
                        jnp.broadcast_to(foot[q : q + 1, :], (SUB, LANES))[None]
                        for q in range(HALO)
                    ],
                    axis=0,
                )
                for b in (1, 0):
                    turned = pltpu.roll(gfe[i, b, :HALO, :, ls], SUB - 1, axis=1)
                    main = gfe[i, b, :, :, ls]
                    late = jnp.where(bottom, after, turned)
                    after = turned
                    total = short_conv(weights, jnp.concatenate([main, late], axis=0), False)
                    op[i, rows[b], ls] = total.reshape(B, LANES).astype(BF16)
                return inner

            lax.fori_loop(0, W // LANES, part_b, 0)
        store_gproj(c).start()
        return carry

    s_sy = sems.take(2 * NY)
    s_az = sems.take(2 * NZ)
    s_ac = sems.take(2)
    s_qx = sems.take(4 * nch)
    s_qz = sems.take(2 * NZ)
    s_qy = sems.take(2 * NY)

    def added(buf, count):
        value = buf[0]
        for k in range(1, count):
            value = value + buf[k]
        return value

    def share(buf, value, spot, base, count, to):
        buf[spot] = value
        place = lambda: buf.at[spot]
        for o in range(1, count):
            send(place, place, base + o, base + count + o, functools.partial(to, o))

    def filter_done():
        for o in range(1, NZ):
            got(frzr.at[o - 1], s_fz + o, s_fz + NZ + o)
        total = frz_f[slab_at(z), :]
        for o in range(1, NZ):
            total = total + frzr[o - 1].astype(F32)
        for e in range(per_device):
            lag = (me * per_device + e).astype(F32)
            value = total[e * cbn : (e + 1) * cbn, :] * jnp.exp(-decay[...] * lag)
            frfin[pl.ds(e * cbn, cbn), :] = value
        whole = frfin[...]
        square = jnp.sum((whole * whole).reshape(slab // SUB, SUB, LANES), axis=0)
        share(sqy, square, y, s_qy, NY, dev_y)

    def shorts_along_y():
        for o in range(1, NZ):
            got(srzr.at[from_z[o]], s_sz + o, s_sz + NZ + o)
        total = srf[z]
        for o in range(1, NZ):
            total = total + srzr[from_z[o]].astype(F32)
        share(sryr, total, y, s_sy, NY, dev_y)

    cuts = [nchunk // 2, nchunk - max(nchunk // 4, 1)]
    lax.fori_loop(0, cuts[0], backward, 0)
    filter_done()
    lax.fori_loop(cuts[0], cuts[1], backward, 0)
    shorts_along_y()
    lax.fori_loop(cuts[1], nchunk, backward, 0)

    for o in range(1, NY):
        got(sryr.at[from_y[o]], s_sy + o, s_sy + NY + o)
    mine = added(sryr, NY)
    ag[core, z] = mine.astype(BF16)
    own = lambda: ag.at[core, z]
    for o in range(1, NZ):
        send(own, own, s_az + o, s_az + NZ + o, functools.partial(dev_z, o))
    for o in range(1, NY):
        got(sqy.at[from_y[o]], s_qy + o, s_qy + NY + o)
    square = added(sqy, NY)
    square = square + jnp.sum((mine * mine).reshape(piece // SUB, SUB, LANES), axis=0)
    spot = ch * 2 + core
    sqx[spot] = square
    place = lambda: sqx.at[spot]
    for o, dc in near:
        base = s_qx + o * 2 + dc
        send(place, place, base, base + 2 * nch, functools.partial(dev_near, o, dc))
    for o, dc in near:
        base = s_qx + o * 2 + dc
        where = from_x[o] * 2 + lax.rem(core + dc, 2)
        got(sqx.at[where], base, base + 2 * nch)
    share(sqz, added(sqx, 2 * nch), z, s_qz, NZ, dev_z)
    for o in range(1, NZ):
        got(ag.at[core, from_z[o]], s_az + o, s_az + NZ + o)
    own_half = lambda: ag.at[core]
    send(own_half, own_half, s_ac, s_ac + 1, dev_c)
    for o in range(1, NZ):
        got(sqz.at[from_z[o]], s_qz + o, s_qz + NZ + o)
    square = added(sqz, NZ)
    sums = jnp.sum(jnp.sum(square, axis=0, keepdims=True), axis=1, keepdims=True)
    channels = cols * nch
    limit = math.sqrt(K * channels + 3 * FK * channels)
    scale = jnp.minimum(1.0, limit / jnp.sqrt(sums))
    for e in range(per_device):
        for cb in range(cbn):
            value = frfin[e * cbn + cb : e * cbn + cb + 1, :] * scale
            filter_out[e : e + 1, cb * LANES : (cb + 1) * LANES] = value
    got(ag.at[other], s_ac, s_ac + 1)
    each = piece // SUB
    for i in range(3):
        for cb in range(cbn):
            g = i * cbn + cb
            value = ag[g // (NZ * each), g // each % NZ, pl.ds(g % each * SUB, SUB), :]
            value = value.astype(F32) * scale
            short_out[i, :, cb * LANES : (cb + 1) * LANES] = value[:FK]

    def finish(c, carry):
        halo_x(c).wait_send()
        halo_g(c).wait_send()
        store_gated(c).wait()
        store_gproj(c).wait()
        return carry

    lax.fori_loop(0, nchunk, finish, 0)
    for make in sends:
        make().wait_send()


def restore(order_t, gated, gproj, short, filt, gated_out, gproj_out, short_out, filt_out):
    gated_out[...] = dot(order_t[...], gated[...]).astype(BF16)
    for i in range(3):
        gproj_out[i] = dot(order_t[...], gproj[i]).astype(BF16)

    @pl.when(pl.program_id(0) == 0)
    def _():
        short_out[...] = short[...]
        filt_out[...] = filt[...]


def shards(nseq, nch, projected, short_taps, filter_taps, decay, cotangent):
    length, cols = cotangent.shape
    per_device = filter_taps.shape[0]
    cbn = cols // LANES
    slab = per_device * cbn
    half = NY * NZ
    piece = 3 * cbn // (2 * NZ) * SUB
    vmem = pltpu.VMEM
    order, order_t, *rest = [jnp.asarray(value) for value in constants(per_device)]
    consts = [order, *rest]
    any_spec = pl.BlockSpec(memory_space=pl.ANY)
    vmem_spec = pl.BlockSpec(memory_space=pltpu.VMEM)
    scratch = [
        vmem((3, length, cols), BF16),
        vmem((length, cols), BF16),
        vmem((3, SUB, cols), BF16),
        vmem((3, 2, R + HALO, SUB, cols), F32),
        vmem((3, 2, R, SUB, cols), F32),
        vmem((2, R, SUB, cols), F32),
        vmem((length, cols), BF16),
        vmem((length, cols), BF16),
        vmem((B, cols), BF16),
        vmem((B, cols), BF16),
        vmem((4, N, cols), F32),
        vmem((2, N, W), F32),
        vmem((2, N, W), BF16),
        vmem((2, N, W), BF16),
        vmem((N, W), F32),
        vmem((K, W), BF16),
        vmem((slab, LANES), BF16),
        vmem((K * cbn, LANES), BF16),
        vmem((K * cbn, LANES), F32),
        vmem((2, 2, R, SUB, W), F32),
        vmem((3, 2, R, SUB, cols), F32),
        vmem((3, SUB, cols), BF16),
        vmem((3, SUB, cols), BF16),
        vmem((length, cols), BF16),
        vmem((3, length, cols), BF16),
        vmem((K * cbn, LANES), F32),
        vmem((half * slab, LANES), BF16),
        vmem((half * slab, LANES), BF16),
        vmem((half * slab, LANES), F32),
        vmem((half * slab, LANES), BF16),
        vmem((NY - 1, NZ * slab, LANES), BF16),
        vmem((NZ * slab, LANES), F32),
        vmem((NZ * slab, LANES), BF16),
        vmem((NZ - 1, slab, LANES), BF16),
        vmem((slab, LANES), F32),
        vmem((3 * cbn * SUB, LANES), F32),
        vmem((NZ * piece, LANES), F32),
        vmem((NZ, piece, LANES), F32),
        vmem((NZ, piece, LANES), BF16),
        vmem((NZ, piece, LANES), BF16),
        vmem((NY, piece, LANES), F32),
        vmem((2, NZ, piece, LANES), BF16),
        vmem((2 * nch, SUB, LANES), F32),
        vmem((NZ, SUB, LANES), F32),
        vmem((NY, SUB, LANES), F32),
        vmem((B, B), BF16),
        vmem((N, N), BF16),
        vmem((N, N), BF16),
        vmem((B, N), BF16),
        vmem((B, N), BF16),
        vmem((B, N), BF16),
        pltpu.SemaphoreType.DMA((SEM_COUNT,)),
    ]
    gated, gproj, short, filt = pl.pallas_call(
        functools.partial(kernel, nseq, nch),
        name="hyena",
        out_shape=(
            jax.ShapeDtypeStruct((length, cols), BF16),
            jax.ShapeDtypeStruct((3, length, cols), BF16),
            jax.ShapeDtypeStruct((3, FK, cols), F32),
            jax.ShapeDtypeStruct((per_device, cols), F32),
        ),
        in_specs=[any_spec, any_spec] + [vmem_spec] * 3 + [any_spec] * len(consts),
        out_specs=(any_spec, any_spec, vmem_spec, vmem_spec),
        scratch_shapes=scratch,
        compiler_params=pltpu.CompilerParams(
            collective_id=0, has_side_effects=True, vmem_limit_bytes=64 * 1000 * 1000
        ),
    )(
        jnp.transpose(projected, (1, 0, 2)),
        cotangent,
        short_taps,
        filter_taps,
        decay.reshape(cbn, LANES),
        *consts,
    )
    flat = pl.BlockSpec((B, cols), lambda b: (b, 0))
    deep = pl.BlockSpec((3, B, cols), lambda b: (0, b, 0))
    whole = lambda array: pl.BlockSpec(array.shape, lambda b: (0,) * array.ndim)
    gated, gproj, short, filt = pl.pallas_call(
        restore,
        name="restore",
        grid=(length // B,),
        out_shape=tuple(
            jax.ShapeDtypeStruct(array.shape, array.dtype) for array in (gated, gproj, short, filt)
        ),
        in_specs=[whole(order_t), flat, deep, whole(short), whole(filt)],
        out_specs=(flat, deep, whole(short), whole(filt)),
    )(order_t, gated, gproj, short, filt)
    return gated, jnp.transpose(gproj, (1, 0, 2)), short, filt


def solution(mesh):
    placed = (P("seq", None, "ch"), P(None, None, "ch"), P("seq", "ch"), P("ch"), P("seq", "ch"))
    nseq, nch = mesh.shape["seq"], mesh.shape["ch"]
    return jax.shard_map(
        functools.partial(shards, nseq, nch),
        mesh=mesh,
        in_specs=placed,
        out_specs=(P("seq", "ch"), P("seq", None, "ch"), P(None, None, "ch"), P("seq", "ch")),
        check_vma=False,
    )
```

```python
import functools
import math

import jax
import jax.numpy as jnp
import ml_dtypes
import numpy as np
from jax import lax
from jax.experimental import pallas as pl
from jax.experimental.pallas import tpu as pltpu
from jax.sharding import PartitionSpec as P

K = 128
FK = 7
HALO = FK - 1
NY = 4
NZ = 8
B = 128
N = 2 * B
W = 512
LANES = 128
SUB = 8
R = B // SUB
F32 = jnp.float32
BF16 = jnp.bfloat16
MESH = pl.DeviceIdType.MESH


def constants(per_device):
    place = np.arange(B)
    time = (place % SUB) * R + place // SUB
    order = np.zeros((B, B))
    order[place, time] = 1.0
    freq = np.concatenate([np.arange(0, B, 2), np.arange(1, B, 2)])
    sign = np.where(freq % 2 == 0, 1.0, -1.0)
    theta = 2.0 * np.pi * (freq + 0.5) / N
    slot = np.arange(K)
    end = slot % per_device
    rest = slot // per_device
    z, y, core = rest % NZ, (rest // NZ) % NY, rest // (NZ * NY)
    tap = ((y * NZ + z) * 2 + core) * per_device + end

    def forward(times):
        angle = theta[:, None] * times[None, :]
        full = np.concatenate([np.cos(angle), -np.sin(angle)], axis=0)
        high = full.astype(ml_dtypes.bfloat16)
        low = (full - high.astype(np.float64)).astype(ml_dtypes.bfloat16)
        return np.concatenate([high, low], axis=1)

    def inverse(times):
        angle = times[:, None] * theta[None, :]
        return np.concatenate([np.cos(angle), -np.sin(angle)], axis=1) * (2.0 / N)

    angle = tap[:, None] * theta[None, :]
    inv_corr = np.concatenate([np.sin(angle) * sign, np.cos(angle) * sign], axis=1) * (2.0 / N)
    as_bf16 = lambda value: np.asarray(value).astype(ml_dtypes.bfloat16)
    return tuple(
        as_bf16(value)
        for value in (
            order,
            order.T,
            forward(time),
            forward(tap),
            inverse(B + time),
            inverse(time),
            inv_corr,
        )
    )


def dot(a, b):
    return jnp.dot(a, b, preferred_element_type=F32)


def twice(value):
    return jnp.concatenate([value, value], axis=0)


def ahead(p, q):
    return [p[0] + q[2], p[1] - q[3], p[2] - q[0], p[3] + q[1]]


def short_conv(weights, full, back):
    total = None
    for j in range(FK):
        start = HALO - j if back else j
        term = weights[j] * full[start : start + R]
        total = term if total is None else total + term
    return total


def lag_sums(sums, grad, full):
    for j in range(FK):
        term = jnp.sum(grad * full[HALO - j : HALO - j + R], axis=0)
        sums[j] = term if sums[j] is None else sums[j] + term


class Sems:
    def __init__(self, ref):
        self.ref, self.used = ref, 0

    def take(self, count):
        first, self.used = self.used, self.used + count
        return first


SEM_COUNT = 256


def kernel(
    nseq,
    nch,
    proj,
    cot,
    short_taps_hbm,
    taps,
    decay,
    order_hbm,
    fwd_hbm,
    fwd_taps_hbm,
    inv_conv_hbm,
    inv_grad_hbm,
    inv_corr_hbm,
    gated_out,
    gproj_out,
    short_out,
    filter_out,
    xn,
    cn,
    xhalo,
    xp,
    feat,
    cotp,
    mx,
    gf,
    hx,
    hg,
    spec,
    hspec,
    prod,
    prod2,
    khat,
    kbf,
    kmine,
    kgather,
    kflat,
    conv,
    gfe,
    ghsend,
    ghrecv,
    og,
    op,
    fr,
    frs,
    frc,
    fry_f,
    fry,
    fryr,
    frz_f,
    frz,
    frzr,
    frfin,
    sr,
    src_,
    srf,
    srb,
    srzr,
    sryr,
    ag,
    sqx,
    sqz,
    sqy,
    short_taps,
    order,
    fwd,
    fwd_taps,
    inv_conv,
    inv_grad,
    inv_corr,
    sem_ref,
):
    consts_hbm = (order_hbm, short_taps_hbm, fwd_hbm, inv_corr_hbm, fwd_taps_hbm, inv_conv_hbm, inv_grad_hbm)
    consts = (order, short_taps, fwd, inv_corr, fwd_taps, inv_conv, inv_grad)
    cols = cot.shape[1]
    nchunk = cols // W
    cbn = cols // LANES
    per_device = taps.shape[0]
    slab = per_device * cbn
    half = NY * NZ
    me = lax.axis_index("seq")
    ch = lax.axis_index("ch")
    core = lax.rem(me, 2)
    z = lax.rem(me // 2, NZ)
    y = me // (2 * NZ)
    other = 1 - core
    seq_at = lambda yy, zz, cc: (yy * NZ + zz) * 2 + cc
    nxt = lax.rem(me + 1, nseq)
    prv = lax.rem(me + nseq - 1, nseq)
    at_z = [lax.rem(z + o, NZ) for o in range(NZ)]
    at_y = [lax.rem(y + o, NY) for o in range(NY)]
    at_x = [lax.rem(ch + o, nch) for o in range(nch)]
    from_z = [lax.rem(z + NZ - o, NZ) for o in range(NZ)]
    from_y = [lax.rem(y + NY - o, NY) for o in range(NY)]
    from_x = [lax.rem(ch + nch - o, nch) for o in range(nch)]
    dev_z = lambda o: (seq_at(y, at_z[o], core), ch)
    dev_y = lambda o: (seq_at(at_y[o], z, core), ch)
    dev_c = (seq_at(y, z, other), ch)
    dev_next, dev_prev = (nxt, ch), (prv, ch)
    sems = Sems(sem_ref)
    sends = []

    def remote(src, dst, send, recv, dev):
        return pltpu.make_async_remote_copy(
            src_ref=src,
            dst_ref=dst,
            send_sem=sem_ref.at[send],
            recv_sem=sem_ref.at[recv],
            device_id=dev,
            device_id_type=MESH,
        )

    def send(src, dst, ss, rs, dev):
        make = lambda: remote(src(), dst(), ss, rs, dev() if callable(dev) else dev)
        make().start()
        sends.append(make)

    def got(dst, ss, rs):
        remote(dst, dst, ss, rs, dev_next).wait_recv()

    s_in = sems.take(2 * nchunk)

    def load(c):
        at = pl.ds(pl.multiple_of(c * W, W), W)
        return (
            pltpu.make_async_copy(proj.at[:, :, at], xn.at[:, :, at], sem_ref.at[s_in + 2 * c]),
            pltpu.make_async_copy(cot.at[:, at], cn.at[:, at], sem_ref.at[s_in + 2 * c + 1]),
        )

    s_const = sems.take(len(consts_hbm))
    const_loads = [
        pltpu.make_async_copy(src, dst, sem_ref.at[s_const + k])
        for k, (src, dst) in enumerate(zip(consts_hbm, consts))
    ]
    for copy in const_loads[:2]:
        copy.start()
    for copy in load(0):
        copy.start()
    for copy in const_loads[2:]:
        copy.start()
    for c in range(1, nchunk):
        for copy in load(c):
            copy.start()

    barrier = pltpu.get_barrier_semaphore()
    near = [(o, dc) for o in range(nch) for dc in range(2) if o or dc]
    dev_near = lambda o, dc: (seq_at(y, z, lax.rem(core + dc, 2)), at_x[o])
    partners = [dev_next, dev_prev]
    partners += [dev_near(o, dc) for o, dc in near]
    partners += [dev_z(o) for o in range(1, NZ)]
    partners += [dev_y(o) for o in range(1, NY)]
    for dev in partners:
        pl.semaphore_signal(barrier, inc=1, device_id=dev, device_id_type=MESH)

    for e in range(per_device):
        lag = (me * per_device + e).astype(F32)
        fall = jnp.exp(-decay[...] * lag)
        for cb in range(cbn):
            row = taps[e : e + 1, cb * LANES : (cb + 1) * LANES]
            kflat[e * cbn + cb : e * cbn + cb + 1, :] = row
        part = pl.ds(e * cbn, cbn)
        kflat[part, :] = kflat[part, :] * fall
    slot = core * half + y * NZ + z
    slot_at = lambda cc, yy, zz: pl.ds(
        pl.multiple_of((cc * half + yy * NZ + zz) * slab, slab), slab
    )
    bundle_at = lambda cc, yy: pl.ds(
        pl.multiple_of((cc * half + yy * NZ) * slab, NZ * slab), NZ * slab
    )
    half_at = lambda cc: pl.ds(pl.multiple_of(cc * half * slab, half * slab), half * slab)
    kmine[...] = kflat[0:slab, :].astype(BF16)
    kgather[slot_at(core, y, z), :] = kmine[...]

    rows = [slice(0, B), slice(B, 2 * B)]
    const_loads[0].wait()

    def reorder(c, carry):
        for copy in load(c):
            copy.wait()
        at = pl.ds(pl.multiple_of(c * W, W), W)
        for b in range(2):
            for i in range(3):
                xp[i, b, HALO:, :, at] = dot(order[...], xn[i, rows[b], at]).reshape(R, SUB, W)
            cotp[b, :, :, at] = dot(order[...], cn[rows[b], at]).reshape(R, SUB, W)
        return carry

    lax.fori_loop(0, nchunk, reorder, 0)

    pl.semaphore_wait(barrier, len(partners))

    s_xh = sems.take(2)
    tail = proj.shape[1] - SUB
    send(lambda: proj.at[:, pl.ds(tail, SUB), :], lambda: xhalo, s_xh, s_xh + 1, dev_next)
    s_kz = sems.take(2 * NZ)
    own_slot = lambda: kgather.at[slot_at(core, y, z)]
    for o in range(1, NZ):
        send(lambda: kmine, own_slot, s_kz + o, s_kz + NZ + o, functools.partial(dev_z, o))
    s_ky = sems.take(2 * NY)
    s_kc = sems.take(2)
    for copy in const_loads[1:]:
        copy.wait()

    def taps_along_y():
        for o in range(1, NZ):
            got(kgather.at[slot_at(core, y, from_z[o])], s_kz + o, s_kz + NZ + o)
        own = lambda: kgather.at[bundle_at(core, y)]
        for o in range(1, NY):
            send(own, own, s_ky + o, s_ky + NY + o, functools.partial(dev_y, o))

    def taps_to_core():
        for o in range(1, NY):
            got(kgather.at[bundle_at(core, from_y[o])], s_ky + o, s_ky + NY + o)
        own = lambda: kgather.at[half_at(core)]
        send(own, own, s_kc, s_kc + 1, dev_c)

    first = jnp.where(me > 0, 1.0, 0.0).astype(F32)
    last = jnp.where(me < nseq - 1, 1.0, 0.0).astype(F32)
    row_id = lax.broadcasted_iota(jnp.int32, (HALO, SUB, LANES), 1)
    top, bottom = row_id == 0, row_id == SUB - 1

    def tap_rows(i, at):
        return [jnp.broadcast_to(short_taps[i, j : j + 1, at], (SUB, LANES)) for j in range(FK)]

    s_hx = sems.take(2 * nchunk)
    s_hg = sems.take(2 * nchunk)

    def halo_x(c):
        at = pl.ds(pl.multiple_of(c * W, W), W)
        return remote(mx.at[pl.ds(B, B), at], hx.at[:, at], s_hx + c, s_hx + nchunk + c, dev_next)

    def halo_g(c):
        at = pl.ds(pl.multiple_of(c * W, W), W)
        return remote(gf.at[pl.ds(0, B), at], hg.at[:, at], s_hg + c, s_hg + nchunk + c, dev_prev)

    def features(b, c, carry):
        at = pl.ds(pl.multiple_of(c * W, W), W)
        if b == 0:

            @pl.when(c == nchunk // 2)
            def _():
                taps_along_y()

        def one(sub, inner):
            ls = pl.ds(pl.multiple_of(c * W + sub * LANES, LANES), LANES)
            feats = []
            for i in range(3):
                weights = tap_rows(i, ls)
                if b == 0:
                    head = xhalo[i, :, ls].astype(F32) * first
                    before = jnp.concatenate(
                        [
                            jnp.broadcast_to(head[2 + q : 3 + q, :], (SUB, LANES))[None]
                            for q in range(HALO)
                        ],
                        axis=0,
                    )
                else:
                    before = pltpu.roll(xp[i, 0, R:, :, ls], 1, axis=1)
                main = xp[i, b, HALO:, :, ls]
                turned = pltpu.roll(main[R - HALO :], 1, axis=1)
                early = jnp.where(top, before, turned)
                xp[i, b, :HALO, :, ls] = early
                total = short_conv(weights, jnp.concatenate([early, main], axis=0), True)
                feat[i, b, :, :, ls] = total
                feats.append(total)
            mx[rows[b], ls] = (feats[1] * feats[2]).reshape(B, LANES).astype(BF16)
            gf[rows[b], ls] = (cotp[b, :, :, ls] * feats[0]).reshape(B, LANES).astype(BF16)
            return inner

        lax.fori_loop(0, W // LANES, one, 0)
        if b == 0:
            halo_g(c).start()
        else:
            halo_x(c).start()
        spec[b, :, at] = dot(fwd[...], twice(mx[rows[b], at]))
        spec[2 + b, :, at] = dot(fwd[...], twice(gf[rows[b], at]))
        return carry

    lax.fori_loop(0, nchunk, functools.partial(features, 1), 0)
    got(xhalo, s_xh, s_xh + 1)
    lax.fori_loop(0, nchunk, functools.partial(features, 0), 0)

    quarter = B // 2

    def quads(ref, rs, ls):
        return [ref[pl.ds(q * quarter + rs, 16), ls] for q in range(4)]

    def correlate(c, carry):
        at = pl.ds(pl.multiple_of(c * W, W), W)
        halo_x(c).wait_recv()
        halo_g(c).wait_recv()
        hspec[0] = dot(fwd[...], twice(hx[:, at]))
        hspec[1] = dot(fwd[...], twice(hg[:, at]))
        def part_c(sub, inner):
            here = pl.ds(pl.multiple_of(sub * LANES, LANES), LANES)
            ls = pl.ds(pl.multiple_of(c * W + sub * LANES, LANES), LANES)
            for rs in range(0, quarter, 16):
                hq = [v * first for v in quads(hspec.at[0], rs, here)]
                gq = [v * last for v in quads(hspec.at[1], rs, here)]
                a, b, ga, gbq = [quads(spec.at[q], rs, ls) for q in range(4)]
                x0, x1 = ahead(hq, a), ahead(a, b)
                g0, g1 = ahead(ga, gbq), ahead(gbq, gq)
                for q in range(4):
                    part = pl.ds(q * quarter + rs, 16)
                    spec[0, part, ls] = x0[q]
                    spec[1, part, ls] = x1[q]
                    spec[2, part, ls] = g0[q]
                    spec[3, part, ls] = g1[q]
                for q in range(2):
                    re = ga[q] * x0[q] + ga[q + 2] * x0[q + 2]
                    re = re + (gbq[q] * x1[q] + gbq[q + 2] * x1[q + 2])
                    im = ga[q + 2] * x0[q] - ga[q] * x0[q + 2]
                    im = im + (gbq[q + 2] * x1[q] - gbq[q] * x1[q + 2])
                    prod[0, pl.ds(q * quarter + rs, 16), here] = re.astype(BF16)
                    prod[0, pl.ds((q + 2) * quarter + rs, 16), here] = im.astype(BF16)
            return inner

        lax.fori_loop(0, W // LANES, part_c, 0)

        @pl.when(c == nchunk - 1)
        def _():
            taps_to_core()

        corr = dot(inv_corr[...], prod[0])
        for sub in range(W // LANES):
            cb = c * (W // LANES) + sub
            fr[pl.ds(cb, K, stride=cbn), :] = corr[:, sub * LANES : (sub + 1) * LANES]
        return carry

    lax.fori_loop(0, nchunk, correlate, 0)

    s_fc = sems.take(2)
    frs[...] = fr[half_at(other), :].astype(BF16)
    send(lambda: frs, lambda: frc, s_fc, s_fc + 1, dev_c)
    got(kgather.at[half_at(other)], s_kc, s_kc + 1)
    kflat[...] = kgather[...].astype(F32)
    s_fy = sems.take(2 * NY)
    s_fz = sems.take(2 * NZ)
    quart = NZ * slab
    quart_at = lambda yy: pl.ds(pl.multiple_of(yy * quart, quart), quart)
    slab_at = lambda zz: pl.ds(pl.multiple_of(zz * slab, slab), slab)

    def filter_along_y():
        got(frc, s_fc, s_fc + 1)
        fry_f[...] = fr[half_at(core), :] + frc[...].astype(F32)
        fry[...] = fry_f[...].astype(BF16)
        for o in range(1, NY):
            source = lambda o=o: fry.at[quart_at(at_y[o])]
            send(source, lambda o=o: fryr.at[o - 1], s_fy + o, s_fy + NY + o, functools.partial(dev_y, o))

    def filter_along_z():
        for o in range(1, NY):
            got(fryr.at[o - 1], s_fy + o, s_fy + NY + o)
        total = fry_f[quart_at(y), :]
        for o in range(1, NY):
            total = total + fryr[o - 1].astype(F32)
        frz_f[...] = total
        frz[...] = total.astype(BF16)
        for o in range(1, NZ):
            source = lambda o=o: frz.at[slab_at(at_z[o])]
            send(source, lambda o=o: frzr.at[o - 1], s_fz + o, s_fz + NZ + o, functools.partial(dev_z, o))

    s_og = sems.take(nchunk)

    def store_gated(c):
        at = pl.ds(pl.multiple_of(c * W, W), W)
        return pltpu.make_async_copy(og.at[:, at], gated_out.at[:, at], sem_ref.at[s_og + c])

    def filters(c, carry):
        at = pl.ds(pl.multiple_of(c * W, W), W)

        @pl.when(c == min(1, nchunk - 1))
        def _():
            filter_along_y()

        for sub in range(W // LANES):
            cb = c * (W // LANES) + sub
            here = slice(sub * LANES, (sub + 1) * LANES)
            kbf[:, here] = kflat[pl.ds(cb, K, stride=cbn), :].astype(BF16)
        khat[...] = dot(fwd_taps[...], twice(kbf[...]))
        def part_p(sub, inner):
            here = pl.ds(pl.multiple_of(sub * LANES, LANES), LANES)
            ls = pl.ds(pl.multiple_of(c * W + sub * LANES, LANES), LANES)
            for rs in range(0, B, 16):
                re, im = pl.ds(rs, 16), pl.ds(B + rs, 16)
                kr, ki = khat[re, here], khat[im, here]
                for b in range(2):
                    xr, xi = spec[b, re, ls], spec[b, im, ls]
                    prod[b, re, here] = (kr * xr - ki * xi).astype(BF16)
                    prod[b, im, here] = (kr * xi + ki * xr).astype(BF16)
                    xr, xi = spec[2 + b, re, ls], spec[2 + b, im, ls]
                    prod2[b, re, here] = (kr * xr + ki * xi).astype(BF16)
                    prod2[b, im, here] = (kr * xi - ki * xr).astype(BF16)
            return inner

        lax.fori_loop(0, W // LANES, part_p, 0)
        for b in range(2):
            conv[0, b] = dot(inv_conv[...], prod[b]).reshape(R, SUB, W)
            conv[1, b] = dot(inv_grad[...], prod2[b]).reshape(R, SUB, W)
        def part_g(sub, inner):
            here = pl.ds(pl.multiple_of(sub * LANES, LANES), LANES)
            ls = pl.ds(pl.multiple_of(c * W + sub * LANES, LANES), LANES)
            zero = jnp.zeros((1, LANES), F32)
            cb = c * (W // LANES) + sub
            sums = [[None] * FK for _ in range(3)]
            for b in range(2):
                filtered, mixed_grad = conv[0, b, :, :, here], conv[1, b, :, :, here]
                gate = feat[0, b, :, :, ls] * filtered
                og[rows[b], ls] = gate.reshape(B, LANES).astype(BF16)
                factors = [
                    (cotp[b, :, :, ls], filtered),
                    (mixed_grad, feat[2, b, :, :, ls]),
                    (mixed_grad, feat[1, b, :, :, ls]),
                ]
                for i, (one, two) in enumerate(factors):
                    grad = one * two
                    gfe[i, b, :, :, ls] = grad
                    lag_sums(sums[i], grad, xp[i, b, :, :, ls])
                    if b == 0:
                        heads = [grad[q, 0:1] for q in range(HALO)]
                        ghsend[i, :, ls] = jnp.concatenate(heads + [zero, zero], axis=0).astype(BF16)
            for i in range(3):
                parts = [jnp.sum(v, axis=0, keepdims=True) for v in sums[i]]
                at_slab = pl.ds(pl.multiple_of((i * cbn + cb) * SUB, SUB), SUB)
                sr[at_slab, :] = jnp.concatenate(parts + [zero], axis=0)
            return inner

        lax.fori_loop(0, W // LANES, part_g, 0)
        store_gated(c).start()
        return carry

    lax.fori_loop(0, nchunk, filters, 0)

    s_sc = sems.take(2)
    shalf = 3 * cbn // 2 * SUB
    piece = shalf // NZ
    shalf_at = lambda cc: pl.ds(pl.multiple_of(cc * shalf, shalf), shalf)
    send(lambda: sr.at[shalf_at(other)], lambda: src_, s_sc, s_sc + 1, dev_c)
    s_gh = sems.take(2)
    send(lambda: ghsend, lambda: ghrecv, s_gh, s_gh + 1, dev_prev)
    s_sz = sems.take(2 * NZ)
    filter_along_z()
    got(src_, s_sc, s_sc + 1)
    srf[...] = (sr[shalf_at(core), :] + src_[...]).reshape(NZ, piece, LANES)
    srb[...] = srf[...].astype(BF16)
    for o in range(1, NZ):
        source = lambda o=o: srb.at[at_z[o]]
        send(source, lambda: srzr.at[z], s_sz + o, s_sz + NZ + o, functools.partial(dev_z, o))

    got(ghrecv, s_gh, s_gh + 1)
    s_op = sems.take(nchunk)

    def store_gproj(c):
        at = pl.ds(pl.multiple_of(c * W, W), W)
        return pltpu.make_async_copy(op.at[:, :, at], gproj_out.at[:, :, at], sem_ref.at[s_op + c])

    def backward(c, carry):
        at = pl.ds(pl.multiple_of(c * W, W), W)
        for i in range(3):
            def part_b(sub, inner, i=i):
                here = pl.ds(pl.multiple_of(sub * LANES, LANES), LANES)
                ls = pl.ds(pl.multiple_of(c * W + sub * LANES, LANES), LANES)
                weights = tap_rows(i, ls)
                foot = ghrecv[i, :, ls].astype(F32) * last
                after = jnp.concatenate(
                    [
                        jnp.broadcast_to(foot[q : q + 1, :], (SUB, LANES))[None]
                        for q in range(HALO)
                    ],
                    axis=0,
                )
                for b in (1, 0):
                    turned = pltpu.roll(gfe[i, b, :HALO, :, ls], SUB - 1, axis=1)
                    main = gfe[i, b, :, :, ls]
                    late = jnp.where(bottom, after, turned)
                    after = turned
                    total = short_conv(weights, jnp.concatenate([main, late], axis=0), False)
                    op[i, rows[b], ls] = total.reshape(B, LANES).astype(BF16)
                return inner

            lax.fori_loop(0, W // LANES, part_b, 0)
        store_gproj(c).start()
        return carry

    s_sy = sems.take(2 * NY)
    s_az = sems.take(2 * NZ)
    s_ac = sems.take(2)
    s_qx = sems.take(4 * nch)
    s_qz = sems.take(2 * NZ)
    s_qy = sems.take(2 * NY)

    def added(buf, count):
        value = buf[0]
        for k in range(1, count):
            value = value + buf[k]
        return value

    def share(buf, value, spot, base, count, to):
        buf[spot] = value
        place = lambda: buf.at[spot]
        for o in range(1, count):
            send(place, place, base + o, base + count + o, functools.partial(to, o))

    def filter_done():
        for o in range(1, NZ):
            got(frzr.at[o - 1], s_fz + o, s_fz + NZ + o)
        total = frz_f[slab_at(z), :]
        for o in range(1, NZ):
            total = total + frzr[o - 1].astype(F32)
        for e in range(per_device):
            lag = (me * per_device + e).astype(F32)
            value = total[e * cbn : (e + 1) * cbn, :] * jnp.exp(-decay[...] * lag)
            frfin[pl.ds(e * cbn, cbn), :] = value
        whole = frfin[...]
        square = jnp.sum((whole * whole).reshape(slab // SUB, SUB, LANES), axis=0)
        share(sqy, square, y, s_qy, NY, dev_y)

    def shorts_along_y():
        for o in range(1, NZ):
            got(srzr.at[from_z[o]], s_sz + o, s_sz + NZ + o)
        total = srf[z]
        for o in range(1, NZ):
            total = total + srzr[from_z[o]].astype(F32)
        share(sryr, total, y, s_sy, NY, dev_y)

    cut = nchunk - max(nchunk // 4, 1)
    lax.fori_loop(0, cut, backward, 0)
    shorts_along_y()
    filter_done()
    lax.fori_loop(cut, nchunk, backward, 0)

    for o in range(1, NY):
        got(sryr.at[from_y[o]], s_sy + o, s_sy + NY + o)
    mine = added(sryr, NY)
    ag[core, z] = mine.astype(BF16)
    own = lambda: ag.at[core, z]
    for o in range(1, NZ):
        send(own, own, s_az + o, s_az + NZ + o, functools.partial(dev_z, o))
    for o in range(1, NY):
        got(sqy.at[from_y[o]], s_qy + o, s_qy + NY + o)
    square = added(sqy, NY)
    square = square + jnp.sum((mine * mine).reshape(piece // SUB, SUB, LANES), axis=0)
    spot = ch * 2 + core
    sqx[spot] = square
    place = lambda: sqx.at[spot]
    for o, dc in near:
        base = s_qx + o * 2 + dc
        send(place, place, base, base + 2 * nch, functools.partial(dev_near, o, dc))
    for o, dc in near:
        base = s_qx + o * 2 + dc
        where = from_x[o] * 2 + lax.rem(core + dc, 2)
        got(sqx.at[where], base, base + 2 * nch)
    share(sqz, added(sqx, 2 * nch), z, s_qz, NZ, dev_z)
    for o in range(1, NZ):
        got(ag.at[core, from_z[o]], s_az + o, s_az + NZ + o)
    own_half = lambda: ag.at[core]
    send(own_half, own_half, s_ac, s_ac + 1, dev_c)
    for o in range(1, NZ):
        got(sqz.at[from_z[o]], s_qz + o, s_qz + NZ + o)
    square = added(sqz, NZ)
    sums = jnp.sum(jnp.sum(square, axis=0, keepdims=True), axis=1, keepdims=True)
    channels = cols * nch
    limit = math.sqrt(K * channels + 3 * FK * channels)
    scale = jnp.minimum(1.0, limit / jnp.sqrt(sums))
    for e in range(per_device):
        for cb in range(cbn):
            value = frfin[e * cbn + cb : e * cbn + cb + 1, :] * scale
            filter_out[e : e + 1, cb * LANES : (cb + 1) * LANES] = value
    got(ag.at[other], s_ac, s_ac + 1)
    each = piece // SUB
    for i in range(3):
        for cb in range(cbn):
            g = i * cbn + cb
            value = ag[g // (NZ * each), g // each % NZ, pl.ds(g % each * SUB, SUB), :]
            value = value.astype(F32) * scale
            short_out[i, :, cb * LANES : (cb + 1) * LANES] = value[:FK]

    def finish(c, carry):
        halo_x(c).wait_send()
        halo_g(c).wait_send()
        store_gated(c).wait()
        store_gproj(c).wait()
        return carry

    lax.fori_loop(0, nchunk, finish, 0)
    for make in sends:
        make().wait_send()


def restore(order_t, gated, gproj, short, filt, gated_out, gproj_out, short_out, filt_out):
    gated_out[...] = dot(order_t[...], gated[...]).astype(BF16)
    for i in range(3):
        gproj_out[i] = dot(order_t[...], gproj[i]).astype(BF16)

    @pl.when(pl.program_id(0) == 0)
    def _():
        short_out[...] = short[...]
        filt_out[...] = filt[...]


def shards(nseq, nch, projected, short_taps, filter_taps, decay, cotangent):
    length, cols = cotangent.shape
    per_device = filter_taps.shape[0]
    cbn = cols // LANES
    slab = per_device * cbn
    half = NY * NZ
    piece = 3 * cbn // (2 * NZ) * SUB
    vmem = pltpu.VMEM
    order, order_t, *rest = [jnp.asarray(value) for value in constants(per_device)]
    consts = [order, *rest]
    any_spec = pl.BlockSpec(memory_space=pl.ANY)
    vmem_spec = pl.BlockSpec(memory_space=pltpu.VMEM)
    scratch = [
        vmem((3, length, cols), BF16),
        vmem((length, cols), BF16),
        vmem((3, SUB, cols), BF16),
        vmem((3, 2, R + HALO, SUB, cols), F32),
        vmem((3, 2, R, SUB, cols), F32),
        vmem((2, R, SUB, cols), F32),
        vmem((length, cols), BF16),
        vmem((length, cols), BF16),
        vmem((B, cols), BF16),
        vmem((B, cols), BF16),
        vmem((4, N, cols), F32),
        vmem((2, N, W), F32),
        vmem((2, N, W), BF16),
        vmem((2, N, W), BF16),
        vmem((N, W), F32),
        vmem((K, W), BF16),
        vmem((slab, LANES), BF16),
        vmem((K * cbn, LANES), BF16),
        vmem((K * cbn, LANES), F32),
        vmem((2, 2, R, SUB, W), F32),
        vmem((3, 2, R, SUB, cols), F32),
        vmem((3, SUB, cols), BF16),
        vmem((3, SUB, cols), BF16),
        vmem((length, cols), BF16),
        vmem((3, length, cols), BF16),
        vmem((K * cbn, LANES), F32),
        vmem((half * slab, LANES), BF16),
        vmem((half * slab, LANES), BF16),
        vmem((half * slab, LANES), F32),
        vmem((half * slab, LANES), BF16),
        vmem((NY - 1, NZ * slab, LANES), BF16),
        vmem((NZ * slab, LANES), F32),
        vmem((NZ * slab, LANES), BF16),
        vmem((NZ - 1, slab, LANES), BF16),
        vmem((slab, LANES), F32),
        vmem((3 * cbn * SUB, LANES), F32),
        vmem((NZ * piece, LANES), F32),
        vmem((NZ, piece, LANES), F32),
        vmem((NZ, piece, LANES), BF16),
        vmem((NZ, piece, LANES), BF16),
        vmem((NY, piece, LANES), F32),
        vmem((2, NZ, piece, LANES), BF16),
        vmem((2 * nch, SUB, LANES), F32),
        vmem((NZ, SUB, LANES), F32),
        vmem((NY, SUB, LANES), F32),
        vmem((3, FK, cols), F32),
        vmem((B, B), BF16),
        vmem((N, N), BF16),
        vmem((N, N), BF16),
        vmem((B, N), BF16),
        vmem((B, N), BF16),
        vmem((B, N), BF16),
        pltpu.SemaphoreType.DMA((SEM_COUNT,)),
    ]
    gated, gproj, short, filt = pl.pallas_call(
        functools.partial(kernel, nseq, nch),
        name="hyena",
        out_shape=(
            jax.ShapeDtypeStruct((length, cols), BF16),
            jax.ShapeDtypeStruct((3, length, cols), BF16),
            jax.ShapeDtypeStruct((3, FK, cols), F32),
            jax.ShapeDtypeStruct((per_device, cols), F32),
        ),
        in_specs=[any_spec, any_spec, any_spec, vmem_spec, vmem_spec] + [any_spec] * len(consts),
        out_specs=(any_spec, any_spec, vmem_spec, vmem_spec),
        scratch_shapes=scratch,
        compiler_params=pltpu.CompilerParams(
            collective_id=0, has_side_effects=True, vmem_limit_bytes=64 * 1000 * 1000
        ),
    )(
        jnp.transpose(projected, (1, 0, 2)),
        cotangent,
        short_taps,
        filter_taps,
        decay.reshape(cbn, LANES),
        *consts,
    )
    flat = pl.BlockSpec((B, cols), lambda b: (b, 0))
    deep = pl.BlockSpec((3, B, cols), lambda b: (0, b, 0))
    whole = lambda array: pl.BlockSpec(array.shape, lambda b: (0,) * array.ndim)
    gated, gproj, short, filt = pl.pallas_call(
        restore,
        name="restore",
        grid=(length // B,),
        out_shape=tuple(
            jax.ShapeDtypeStruct(array.shape, array.dtype) for array in (gated, gproj, short, filt)
        ),
        in_specs=[whole(order_t), flat, deep, whole(short), whole(filt)],
        out_specs=(flat, deep, whole(short), whole(filt)),
    )(order_t, gated, gproj, short, filt)
    return gated, jnp.transpose(gproj, (1, 0, 2)), short, filt


def solution(mesh):
    placed = (P("seq", None, "ch"), P(None, None, "ch"), P("seq", "ch"), P("ch"), P("seq", "ch"))
    nseq, nch = mesh.shape["seq"], mesh.shape["ch"]
    return jax.shard_map(
        functools.partial(shards, nseq, nch),
        mesh=mesh,
        in_specs=placed,
        out_specs=(P("seq", "ch"), P("seq", None, "ch"), P(None, None, "ch"), P("seq", "ch")),
        check_vma=False,
    )
```
